256 devices in a mesh: dp: 4 (over y), cp: 64 (over x, z, core).
Axes of the slice: x: 4, y: 4, z: 8, core: 2. Of those that a mesh axis runs over, the one named last changes fastest.
Arguments:
- query_rows: bfloat16 [32768, 4096], P(('dp', 'cp')), parts along dimension 0, may hold values from -90 to 90
- key_rows: bfloat16 [32768, 512], P(('dp', 'cp')), parts along dimension 0, may hold values from -5 to 5
- value_rows: bfloat16 [32768, 512], P(('dp', 'cp')), parts along dimension 0, may hold values from -6 to 6
- gate_rows: bfloat16 [32768, 4096], P(('dp', 'cp')), parts along dimension 0, may hold values from -6 to 6
- doc_ids: int32 [32768], P(('dp', 'cp')), parts along dimension 0, may hold values from 0 to 15, never falling along the last dimension, each value on 1 to 4096 neighbouring positions
- block_lists: int32 [256, 64], P(('dp', 'cp')), parts along dimension 0, may hold values from 0 to 1, as said below
Outputs:
- gated_attention: bfloat16 [32768, 4096], P(('dp', 'cp')), parts along dimension 0
The draws below stay inside these ranges and needn't reach their ends.
There are 4 independent parts, one for each index of `dp`. The reference program is written for one: setup_inputs(seed, part) draws one part's arguments, and reference() takes and returns one part's arrays. A program takes and returns all parts, laid end to end along the dimension named above; each array names one. Nothing has to cross between parts.
Inputs may be any that keep to these rules, and one draw needn't show every extreme that they name: `block_lists`: row q has a 1 at column q and only zeros at columns above q.
All inputs are finite; a program needn't handle non-finite values.
Results may differ from the reference program's by a relative error of at most 0.0038.
Values may be sent and summed in bfloat16 or wider, within the bound.
No kernel may reach another device: no remote copies, remote signals or barrier semaphores. Data moves between devices by JAX's collectives and lax.ppermute only.
A program may use at most 128 MiB of HBM per device.

```python
import math
import jax
import jax.numpy as jnp
import numpy as np
from jax import lax

H = 16
KVH = 2
HD = 256
BLK = 128
SEQ = 8192
N_CP = 64


def make_pair(key):
    groups = H // KVH
    key_rows = jnp.clip(jax.random.normal(jax.random.fold_in(key, 202), (SEQ, KVH, HD), jnp.float32), -5.0, 5.0)
    query_rows = jnp.clip(jax.random.normal(jax.random.fold_in(key, 101), (SEQ, KVH, groups, HD), jnp.float32), -5.0, 5.0)
    return (query_rows.reshape(SEQ, H * HD), key_rows.reshape(SEQ, KVH * HD))


def draw_query_rows(key, part):
    return make_pair(key)[0].astype(jnp.bfloat16)


def draw_key_rows(key, part):
    return make_pair(key)[1].astype(jnp.bfloat16)


def draw_block_lists(key, part):
    num_blocks = SEQ // BLK
    coin = jax.random.randint(jax.random.fold_in(key, 505), (num_blocks, num_blocks), 0, 20) < 17
    row_ids = jnp.arange(num_blocks, dtype=jnp.int32)[:, None]
    col_ids = jnp.arange(num_blocks, dtype=jnp.int32)[None, :]
    lower = (col_ids < row_ids) & coin
    return jnp.where((col_ids == row_ids) | lower, 1, 0).astype(jnp.int32)


def shard_levels(rng, shape, split, smallest, largest):
    def one(dim, blocks):
        draws = jax.random.uniform(jax.random.fold_in(jax.random.fold_in(rng, 6), dim), (blocks,), jnp.float32, smallest / len(split), largest / len(split))
        return jnp.repeat(jnp.exp(draws), shape[dim] // blocks).reshape((-1,) + (1,) * (len(shape) - dim - 1))

    level = one(*split[0])
    for cut in split[1:]:
        level = level * one(*cut)
    return level


def length_profile(number_of, total, limit, lean):
    portions = [(1 << 20) // math.isqrt(rank ** lean) + 1 for rank in range(2, number_of + 1)]
    surplus, counts = total - limit - (number_of - 1), [1] * (number_of - 1)
    while surplus > 0:
        free = [i for i in range(number_of - 1) if counts[i] < limit]
        mass, remaining = sum([portions[i] for i in free]), surplus
        for i in free:
            more = min(limit - counts[i], max(1, remaining * portions[i] // mass), surplus)
            counts[i] = counts[i] + more
            surplus = surplus - more
    return np.array([limit] + counts)


def ragged_sizes(stream_key, number_of, total, reach, slope):
    if number_of == 2:
        one = jax.random.randint(stream_key, (), max(1, total - reach), min(reach, total - 1) + 1)
        return jnp.stack([one, total - one])
    lengths = jnp.asarray(length_profile(number_of, total, reach, slope), jnp.int32)
    twos = (number_of - 1) // 2
    donor, taker = lengths[1:1 + 2 * twos:2], lengths[2:2 + 2 * twos:2]
    slack = jnp.minimum(donor - 1, reach - taker)
    moved = jax.random.randint(jax.random.fold_in(stream_key, 1), (twos,), 0, 1 << 20) % (slack + 1)
    lengths = lengths.at[1:1 + 2 * twos:2].set(donor - moved).at[2:2 + 2 * twos:2].set(taker + moved)
    return lengths[jax.random.permutation(jax.random.fold_in(stream_key, 2), number_of)]


def bell_draw(stream_key, dims, deviation, limit, cuts=(), kind=jnp.bfloat16):
    values = jax.random.normal(stream_key, dims, jnp.float32) * deviation
    if len(cuts) > 0:
        values = shard_levels(stream_key, dims, cuts, -0.22, 0.18) * values
    return jnp.clip(values, min=-limit, max=limit).astype(kind)


def setup_inputs(seed: int = 0, part: int = 0) -> dict:
    streams_of = jax.random.split(jax.random.key(seed), 7)
    part_splits = jax.random.split(jax.random.fold_in(streams_of[6], part), 7)
    query_rows = draw_query_rows(jax.random.fold_in(jax.random.fold_in(streams_of[6], part), 71), part)
    key_rows = draw_key_rows(jax.random.fold_in(jax.random.fold_in(streams_of[6], part), 71), part)
    value_rows = bell_draw(part_splits[2], (SEQ, KVH * HD), 1.0, 6.0, ((0, 64),))
    gate_rows = bell_draw(part_splits[3], (SEQ, H * HD), 1.5, 6.0, ((0, 64),))
    doc_ids = jnp.searchsorted(jnp.cumsum(ragged_sizes(part_splits[4], max(2, N_CP // 4), SEQ, SEQ // 2, 2)), jnp.arange(SEQ), side="right").astype(jnp.int32)
    block_lists = draw_block_lists(jax.random.fold_in(jax.random.fold_in(streams_of[6], part), 71), part)
    return dict(query_rows=query_rows, key_rows=key_rows, value_rows=value_rows, gate_rows=gate_rows, doc_ids=doc_ids, block_lists=block_lists)


def reference(query_rows, key_rows, value_rows, gate_rows, doc_ids, block_lists):
    num_blocks = SEQ // BLK
    groups = H // KVH
    scale_factor = 1.0 / math.sqrt(HD)
    queries_full = query_rows.astype(jnp.float32).reshape(num_blocks, BLK, KVH, groups, HD)
    keys_full = key_rows.astype(jnp.float32).reshape(num_blocks, BLK, KVH, HD)
    values_full = value_rows.astype(jnp.float32).reshape(num_blocks, BLK, KVH, HD)
    gates_full = gate_rows.astype(jnp.float32).reshape(num_blocks, BLK, H * HD)
    docs_full = doc_ids.reshape(num_blocks, BLK)
    block_ids = jnp.arange(num_blocks, dtype=jnp.int32)
    offsets = jnp.arange(BLK, dtype=jnp.int32)

    def one_block(inputs):
        query_block, gate_block, query_docs, list_row, query_index = inputs
        query_pos = query_index * BLK + offsets

        def visibility(key_docs, key_index, listed):
            key_pos = key_index * BLK + offsets
            return (key_pos[None, :] <= query_pos[:, None]) & (key_docs[None, :] == query_docs[:, None]) & (listed == 1)

        def scores_of(key_block, visible):
            scores = jnp.einsum('rkgd,nkd->kgrn', query_block, key_block) * scale_factor
            return jnp.where(visible[None, None], scores, -1e+30)

        def max_step(best, items):
            key_block, key_docs, key_index, listed = items
            visible = visibility(key_docs, key_index, listed)

            def compute(current):
                return jnp.maximum(current, lax.optimization_barrier(jnp.max(scores_of(key_block, visible), axis=-1)))
            return (lax.cond(jnp.any(visible), compute, lambda current: current, best), None)
        start_best = jnp.full((KVH, groups, BLK), -1e+30, jnp.float32)
        best, _ = lax.scan(max_step, start_best, (keys_full, docs_full, block_ids, list_row))

        def sum_step(state, items):
            key_block, value_block, key_docs, key_index, listed = items
            visible = visibility(key_docs, key_index, listed)

            def compute(inner):
                total, weighted = inner
                scores = scores_of(key_block, visible)
                weights = jnp.where(visible[None, None], jnp.exp(scores - best[..., None]), 0.0)
                rounded = lax.optimization_barrier(weights.astype(jnp.bfloat16)).astype(jnp.float32)
                return (total + lax.optimization_barrier(jnp.sum(weights, axis=-1)), weighted + jnp.einsum('kgrn,nkd->kgrd', rounded, value_block))
            return (lax.cond(jnp.any(visible), compute, lambda inner: inner, state), None)
        start_state = (jnp.zeros((KVH, groups, BLK), jnp.float32), jnp.zeros((KVH, groups, BLK, HD), jnp.float32))
        (total, weighted), _ = lax.scan(sum_step, start_state, (keys_full, values_full, docs_full, block_ids, list_row))
        result = jnp.transpose(weighted / total[..., None], (2, 0, 1, 3)).reshape(BLK, H * HD)
        return (result * jax.nn.sigmoid(gate_block)).astype(jnp.bfloat16)
    blocks_out = lax.map(one_block, (queries_full, gates_full, docs_full, block_lists, block_ids))
    return blocks_out.reshape(SEQ, H * HD)
```

```python
import functools
import math

import jax
import jax.numpy as jnp
from jax import lax
from jax.experimental import pallas as pl
from jax.experimental.pallas import tpu as pltpu
from jax.sharding import PartitionSpec as P

H = 16
KVH = 2
HD = 256
BLK = 128
GROUPS = H // KVH
NX, NZ = 4, 8
UNIT = 2 * BLK
META = 16
ROWS = GROUPS * UNIT
HALF = GROUPS * HD
LOG2E = 1.4426950408889634
NEG = -1e30


def permutation(target):
    pairs = []
    for x in range(NX):
        for z in range(NZ):
            for core in range(2):
                goal = target(x, z, core)
                if goal is not None:
                    gx, gz, gc = goal
                    pairs.append(((x * NZ + z) * 2 + core, (gx * NZ + gz) * 2 + gc))
    return pairs


SWAP = permutation(lambda x, z, c: (x, z, 1 - c))
ONE_X = permutation(lambda x, z, c: (x + 1, z, c) if x < 3 else None)
TWO_X = permutation(lambda x, z, c: ((x + 2) % NX, z, c))
NEAR_UP = permutation(
    lambda x, z, c: (x, z + 1, c) if z < 7 else ((x + 2, 0, c) if x < 2 else None)
)
NEAR_DOWN = permutation(
    lambda x, z, c: (x, z - 1, c) if z > 0 else ((x + 2) % NX, 7, c)
)
MID_UP = permutation(lambda x, z, c: (x, (z + 1) % NZ, c) if x > 0 else None)
MID_DOWN = permutation(lambda x, z, c: (x, (z - 1) % NZ, c) if x > 0 else None)


def attend(own_at, last, count, *refs):
    flags, core, q, qdocs = refs[:4]
    units = refs[4 : 4 + count]
    rest = list(refs[4 + count :])
    first = own_at is not None
    if not first:
        m_in, l_in, acc_in = rest[:3]
        rest = rest[3:]
    if last:
        gate_mine, gate_other = rest[:2]
        rest = rest[2:]
        out_mine, out_other = rest[:2]
    else:
        m_out, l_out, acc_out = rest[:3]
        rest = rest[3:]
    me = core[0]
    lane = lax.broadcasted_iota(jnp.int32, (1, UNIT), 1)
    biases = []
    for j in range(count):
        kd = units[j][UNIT : UNIT + META, :].astype(jnp.float32)[0:1, :]
        halves = []
        for r in range(2):
            listed = jnp.where(lane < BLK, flags[j, 2 * r], flags[j, 2 * r + 1])
            kd_r = jnp.where(listed == 1, kd, -1.0)
            qd = qdocs[r * BLK : (r + 1) * BLK, :]
            qd = jnp.concatenate([qd, qd], axis=1)
            seen = qd == kd_r
            if own_at == j:
                col = lax.broadcasted_iota(jnp.int32, (BLK, UNIT), 1)
                row = lax.broadcasted_iota(jnp.int32, (BLK, UNIT), 0)
                low = jnp.where(me == 0, col, lax.rem(col + BLK, UNIT))
                place = row + jnp.where(me == r, 0, BLK)
                seen = seen & (low <= place)
            halves.append(jnp.where(seen, 0.0, NEG))
        biases.append(jnp.concatenate(halves, axis=0))
    scale = LOG2E / math.sqrt(HD)
    for h in range(GROUPS):
        qh = q[h * UNIT : (h + 1) * UNIT, :]
        scores = []
        for j in range(count):
            s = lax.dot_general(
                qh,
                units[j][0:UNIT, :],
                (((1,), (1,)), ((), ())),
                preferred_element_type=jnp.float32,
            )
            scores.append(s * scale + biases[j])
        top = scores[0]
        for s in scores[1:]:
            top = jnp.maximum(top, s)
        top = jnp.max(top, axis=1, keepdims=True)
        if first:
            m_new = jnp.broadcast_to(top, (UNIT, BLK))
        else:
            m_old = m_in[h]
            m_new = jnp.maximum(m_old, top)
            alpha = jnp.exp2(m_old - m_new)
        m_wide = jnp.concatenate([m_new, m_new], axis=1)
        total = None
        product = None
        for j in range(count):
            p = jnp.exp2(scores[j] - m_wide)
            part = p[:, :BLK] + p[:, BLK:]
            total = part if total is None else total + part
            pv = jnp.dot(
                p.astype(jnp.bfloat16),
                units[j][UNIT + META :, :],
                preferred_element_type=jnp.float32,
            )
            product = pv if product is None else product + pv
        if not first:
            total = total + alpha * l_in[h]
            wide = jnp.concatenate([alpha, alpha], axis=1)
            product = product + wide * acc_in[h]
        if last:
            inv = 1.0 / jnp.sum(total, axis=1, keepdims=True)
            att = product * inv
            base = pl.multiple_of(me * HALF + h * HD, HD)
            g = gate_mine[:, pl.ds(base, HD)].astype(jnp.float32)
            out_mine[:, h * HD : (h + 1) * HD] = (
                att[:BLK] * jax.nn.sigmoid(g)
            ).astype(jnp.bfloat16)
            g = gate_other[:, h * HD : (h + 1) * HD].astype(jnp.float32)
            out_other[:, h * HD : (h + 1) * HD] = (
                att[BLK:] * jax.nn.sigmoid(g)
            ).astype(jnp.bfloat16)
        else:
            m_out[h] = m_new
            l_out[h] = total
            acc_out[h] = product


def attend_call(core, flags, q, qdocs, units, state=None, gates=None, own_at=None):
    count = len(units)
    last = gates is not None
    smem = pl.BlockSpec(memory_space=pltpu.SMEM)
    vmem = pl.BlockSpec(memory_space=pltpu.VMEM)
    args = [flags, core, q, qdocs, *units]
    aliases = {}
    if state is not None:
        if not last:
            aliases = {len(args) + i: i for i in range(3)}
        args += list(state)
    if last:
        args += list(gates)
        shapes = [jax.ShapeDtypeStruct((BLK, HALF), jnp.bfloat16)] * 2
    else:
        shapes = [
            jax.ShapeDtypeStruct((GROUPS, UNIT, BLK), jnp.float32),
            jax.ShapeDtypeStruct((GROUPS, UNIT, BLK), jnp.float32),
            jax.ShapeDtypeStruct((GROUPS, UNIT, HD), jnp.float32),
        ]
    specs = [smem, smem] + [vmem] * (len(args) - 2)
    return pl.pallas_call(
        functools.partial(attend, own_at, last, count),
        out_shape=shapes,
        in_specs=specs,
        out_specs=[vmem] * len(shapes),
        input_output_aliases=aliases,
        compiler_params=pltpu.CompilerParams(vmem_limit_bytes=32 << 20),
        cost_estimate=pl.CostEstimate(
            flops=4 * ROWS * UNIT * HD * count,
            bytes_accessed=count * 270000 + 9000000,
            transcendentals=ROWS * UNIT * count,
        ),
    )(*args)


def on_device(query_rows, key_rows, value_rows, gate_rows, doc_ids, block_lists):
    place = lax.axis_index("cp")
    core = lax.rem(place, 2)
    chip = place // 2
    x, z = chip // NZ, lax.rem(chip, NZ)

    def send(value, pairs):
        return lax.ppermute(value, "cp", pairs)

    def take(rows, which, width):
        return lax.dynamic_slice_in_dim(rows, which * width, width, 1)

    docs_row = doc_ids.astype(jnp.bfloat16).reshape(1, BLK)
    lists_row = jnp.pad(
        block_lists.astype(jnp.bfloat16), ((0, 0), (0, BLK - block_lists.shape[1]))
    )
    notes = jnp.concatenate(
        [docs_row, lists_row, jnp.zeros((META - 2, BLK), jnp.bfloat16)], axis=0
    )
    notes_wide = jnp.concatenate([notes, jnp.zeros_like(notes)], axis=1)
    parcel = jnp.concatenate(
        [take(key_rows, 1 - core, HD), take(value_rows, 1 - core, HD), notes_wide], axis=0
    )
    got = send(parcel, SWAP)
    unit = jnp.concatenate(
        [
            take(key_rows, core, HD),
            got[:BLK],
            jnp.concatenate([notes, got[2 * BLK :, :BLK]], axis=1),
            take(value_rows, core, HD),
            got[BLK : 2 * BLK],
        ],
        axis=0,
    )
    up = [unit]
    mid0 = send(unit, ONE_X)
    low0 = send(unit, TWO_X)
    down = [low0]
    mup, mdown = [mid0], [mid0]
    for s in range(4):
        up.append(send(up[-1], NEAR_UP))
        mup.append(send(mup[-1], MID_UP))
        if s < 3:
            down.append(send(down[-1], NEAR_DOWN))
            mdown.append(send(mdown[-1], MID_DOWN))

    q_other = send(take(query_rows, 1 - core, HALF), SWAP)
    gate_other = send(take(gate_rows, 1 - core, HALF), SWAP)
    q = jnp.concatenate([take(query_rows, core, HALF), q_other], axis=0)
    q = q.reshape(UNIT, GROUPS, HD).transpose(1, 0, 2).reshape(ROWS, HD)
    meta = unit[UNIT : UNIT + 2].astype(jnp.float32)
    qdocs = jnp.broadcast_to(meta[0][:, None], (UNIT, BLK))
    lists = jnp.stack([meta[1, :64], meta[1, BLK : BLK + 64]])

    def up_id(s):
        return jnp.where(z >= s, chip - s, jnp.where(x >= 2, chip - s - NZ, -1))

    def down_id(s):
        return jnp.where(
            z + s < NZ, jnp.where(x >= 2, chip - 2 * NZ + s, -1), chip + s - NZ
        )

    def mid_id(s):
        return jnp.where(x >= 1, (x - 1) * NZ + lax.rem(z + s + NZ, NZ), -1)

    groups = [
        [(up[0], chip)],
        [(up[1], up_id(1)), (down[0], down_id(0)), (mup[0], mid_id(0))],
        [(up[2], up_id(2)), (down[1], down_id(1)), (mup[1], mid_id(-1)), (mdown[1], mid_id(1))],
        [(up[3], up_id(3)), (down[2], down_id(2)), (mup[2], mid_id(-2)), (mdown[2], mid_id(2))],
        [
            (up[4], up_id(4)),
            (down[3], down_id(3)),
            (mup[3], mid_id(-3)),
            (mdown[3], mid_id(3)),
            (mup[4], mid_id(-4)),
        ],
    ]
    ids = jnp.stack([i for group in groups for _, i in group])
    cols = 2 * ids[:, None] + jnp.stack([core, 1 - core])[None, :]
    cols = jnp.where(ids[:, None] >= 0, cols, -1)
    hot = cols[:, None, :, None] == jnp.arange(64, dtype=jnp.int32)[None, None, None, :]
    table = jnp.sum(jnp.where(hot, lists[None, :, None, :], 0.0), axis=-1)
    table = table.astype(jnp.int32).reshape(ids.shape[0], 4)

    core1 = core.reshape(1)
    state = None
    at = 0
    for n, group in enumerate(groups):
        flags = table[at : at + len(group)]
        at += len(group)
        gates = (gate_rows, gate_other) if n == len(groups) - 1 else None
        state = attend_call(
            core1, flags, q, qdocs, [u for u, _ in group], state, gates, 0 if n == 0 else None
        )
    mine, other = state
    back = send(other, SWAP)
    return jnp.where(
        core == 0,
        jnp.concatenate([mine, back], axis=1),
        jnp.concatenate([back, mine], axis=1),
    )


def solution(mesh):
    return jax.shard_map(
        on_device,
        mesh=mesh,
        in_specs=(
            P(("dp", "cp"), None),
            P(("dp", "cp"), None),
            P(("dp", "cp"), None),
            P(("dp", "cp"), None),
            P(("dp", "cp")),
            P(("dp", "cp"), None),
        ),
        out_specs=P(("dp", "cp"), None),
        check_vma=False,
    )
```

```python
import functools
import math

import jax
import jax.numpy as jnp
from jax import lax
from jax.experimental import pallas as pl
from jax.experimental.pallas import tpu as pltpu
from jax.sharding import PartitionSpec as P

H = 16
KVH = 2
HD = 256
BLK = 128
GROUPS = H // KVH
NX, NZ = 4, 8
UNIT = 2 * BLK
META = 16
ROWS = GROUPS * UNIT
HALF = GROUPS * HD
LOG2E = 1.4426950408889634
NEG = -1e30


def pairs_of(links):
    return [(2 * a + c, 2 * b + c) for a, b in sorted(links) for c in range(2)]


def chain_plan(offset, step, length):
    count = NX * NZ

    def seen_by(chip, s):
        unit = chip + offset - step * s
        return 0 <= unit <= chip

    wanted = [set() for _ in range(length + 1)]
    for s in range(length, -1, -1):
        wanted[s] |= {u for u in range(count) if seen_by(u, s)}
        if s:
            wanted[s - 1] |= {(u - step) % count for u in wanted[s]}
    hops = [pairs_of({((u + offset) % count, u) for u in wanted[0]})]
    for s in range(1, length + 1):
        hops.append(pairs_of({((u - step) % count, u) for u in wanted[s]}))
    return hops


def joined(*hops):
    return sorted(set().union(*[set(h) for h in hops]))


SWAP = [(i, i ^ 1) for i in range(2 * NX * NZ)]
NEAR_UP = chain_plan(0, 1, 4)
MID_UP = chain_plan(-NZ, 1, 4)
MID_DOWN = chain_plan(-NZ, -1, 3)
FAR_DOWN = chain_plan(-2 * NZ, -1, 3)


def attend(own_at, last, count, *refs):
    flags, core, q, qdocs = refs[:4]
    units = refs[4 : 4 + count]
    rest = list(refs[4 + count :])
    first = own_at is not None
    if not first:
        m_in, l_in, acc_in = rest[:3]
        rest = rest[3:]
    if last:
        gate_mine, gate_other = rest[:2]
        rest = rest[2:]
        out_mine, out_other = rest[:2]
    else:
        m_out, l_out, acc_out = rest[:3]
        rest = rest[3:]
    me = core[0]
    lane = lax.broadcasted_iota(jnp.int32, (1, UNIT), 1)
    biases = []
    for j in range(count):
        kd = units[j][UNIT : UNIT + META, :].astype(jnp.float32)[0:1, :]
        halves = []
        for r in range(2):
            listed = jnp.where(lane < BLK, flags[j, 2 * r], flags[j, 2 * r + 1])
            kd_r = jnp.where(listed == 1, kd, -1.0)
            qd = qdocs[r * BLK : (r + 1) * BLK, :]
            qd = jnp.concatenate([qd, qd], axis=1)
            seen = qd == kd_r
            if own_at == j:
                col = lax.broadcasted_iota(jnp.int32, (BLK, UNIT), 1)
                row = lax.broadcasted_iota(jnp.int32, (BLK, UNIT), 0)
                low = jnp.where(me == 0, col, lax.rem(col + BLK, UNIT))
                place = row + jnp.where(me == r, 0, BLK)
                seen = seen & (low <= place)
            halves.append(jnp.where(seen, 0.0, NEG))
        biases.append(jnp.concatenate(halves, axis=0))
    scale = LOG2E / math.sqrt(HD)
    for h in range(GROUPS):
        qh = q[h * UNIT : (h + 1) * UNIT, :]
        scores = []
        for j in range(count):
            s = lax.dot_general(
                qh,
                units[j][0:UNIT, :],
                (((1,), (1,)), ((), ())),
                preferred_element_type=jnp.float32,
            )
            scores.append(s * scale + biases[j])
        top = scores[0]
        for s in scores[1:]:
            top = jnp.maximum(top, s)
        top = jnp.max(top, axis=1, keepdims=True)
        if first:
            m_new = jnp.broadcast_to(top, (UNIT, BLK))
        else:
            m_old = m_in[h]
            m_new = jnp.maximum(m_old, top)
            alpha = jnp.exp2(m_old - m_new)
        m_wide = jnp.concatenate([m_new, m_new], axis=1)
        total = None
        product = None
        for j in range(count):
            p = jnp.exp2(scores[j] - m_wide)
            part = p[:, :BLK] + p[:, BLK:]
            total = part if total is None else total + part
            pv = jnp.dot(
                p.astype(jnp.bfloat16),
                units[j][UNIT + META :, :],
                preferred_element_type=jnp.float32,
            )
            product = pv if product is None else product + pv
        if not first:
            total = total + alpha * l_in[h]
            wide = jnp.concatenate([alpha, alpha], axis=1)
            product = product + wide * acc_in[h]
        if last:
            inv = 1.0 / jnp.sum(total, axis=1, keepdims=True)
            att = product * inv
            base = pl.multiple_of(me * HALF + h * HD, HD)
            g = gate_mine[:, pl.ds(base, HD)].astype(jnp.float32)
            out_mine[:, h * HD : (h + 1) * HD] = (
                att[:BLK] * jax.nn.sigmoid(g)
            ).astype(jnp.bfloat16)
            g = gate_other[:, h * HD : (h + 1) * HD].astype(jnp.float32)
            out_other[:, h * HD : (h + 1) * HD] = (
                att[BLK:] * jax.nn.sigmoid(g)
            ).astype(jnp.bfloat16)
        else:
            m_out[h] = m_new
            l_out[h] = total
            acc_out[h] = product


def attend_call(core, flags, q, qdocs, units, state=None, gates=None, own_at=None):
    count = len(units)
    last = gates is not None
    smem = pl.BlockSpec(memory_space=pltpu.SMEM)
    vmem = pl.BlockSpec(memory_space=pltpu.VMEM)
    args = [flags, core, q, qdocs, *units]
    aliases = {}
    if state is not None:
        if not last:
            aliases = {len(args) + i: i for i in range(3)}
        args += list(state)
    if last:
        args += list(gates)
        shapes = [jax.ShapeDtypeStruct((BLK, HALF), jnp.bfloat16)] * 2
    else:
        shapes = [
            jax.ShapeDtypeStruct((GROUPS, UNIT, BLK), jnp.float32),
            jax.ShapeDtypeStruct((GROUPS, UNIT, BLK), jnp.float32),
            jax.ShapeDtypeStruct((GROUPS, UNIT, HD), jnp.float32),
        ]
    specs = [smem, smem] + [vmem] * (len(args) - 2)
    return pl.pallas_call(
        functools.partial(attend, own_at, last, count),
        out_shape=shapes,
        in_specs=specs,
        out_specs=[vmem] * len(shapes),
        input_output_aliases=aliases,
        compiler_params=pltpu.CompilerParams(vmem_limit_bytes=32 << 20),
        cost_estimate=pl.CostEstimate(
            flops=4 * ROWS * UNIT * HD * count,
            bytes_accessed=count * 270000 + 9000000,
            transcendentals=ROWS * UNIT * count,
        ),
    )(*args)


def on_device(query_rows, key_rows, value_rows, gate_rows, doc_ids, block_lists):
    place = lax.axis_index("cp")
    core = lax.rem(place, 2)
    chip = place // 2
    x, z = chip // NZ, lax.rem(chip, NZ)

    def send(value, pairs):
        return lax.ppermute(value, "cp", pairs)

    def take(rows, which, width):
        return lax.dynamic_slice_in_dim(rows, which * width, width, 1)

    docs_row = doc_ids.astype(jnp.bfloat16).reshape(1, BLK)
    lists_row = jnp.pad(
        block_lists.astype(jnp.bfloat16), ((0, 0), (0, BLK - block_lists.shape[1]))
    )
    notes = jnp.concatenate(
        [docs_row, lists_row, jnp.zeros((META - 2, BLK), jnp.bfloat16)], axis=0
    )
    notes_wide = jnp.concatenate([notes, jnp.zeros_like(notes)], axis=1)
    parcel = jnp.concatenate(
        [take(key_rows, 1 - core, HD), take(value_rows, 1 - core, HD), notes_wide], axis=0
    )
    got = send(parcel, SWAP)
    unit = jnp.concatenate(
        [
            take(key_rows, core, HD),
            got[:BLK],
            jnp.concatenate([notes, got[2 * BLK :, :BLK]], axis=1),
            take(value_rows, core, HD),
            got[BLK : 2 * BLK],
        ],
        axis=0,
    )
    near = [unit, send(unit, NEAR_UP[1])]
    mid = [send(unit, joined(MID_UP[0], MID_DOWN[0]))]
    far = [send(unit, FAR_DOWN[0])]
    back_mid = [mid[0]]
    rings = (near, NEAR_UP), (mid, MID_UP), (back_mid, MID_DOWN), (far, FAR_DOWN)

    def advance(s):
        for chain, hops in rings:
            if len(chain) == s and s < len(hops):
                chain.append(send(chain[-1], hops[s]))

    q_other = send(take(query_rows, 1 - core, HALF), SWAP)
    gate_other = send(take(gate_rows, 1 - core, HALF), SWAP)
    q = jnp.concatenate([take(query_rows, core, HALF), q_other], axis=0)
    q = q.reshape(UNIT, GROUPS, HD).transpose(1, 0, 2).reshape(ROWS, HD)
    meta = unit[UNIT : UNIT + 2].astype(jnp.float32)
    qdocs = jnp.broadcast_to(meta[0][:, None], (UNIT, BLK))
    lists = jnp.stack([meta[1, :64], meta[1, BLK : BLK + 64]])

    steps = [
        [(near, 0, chip)],
        [(near, 1, chip - 1), (mid, 0, chip - 8), (far, 0, chip - 16)],
    ]
    for s in range(1, 4):
        steps.append(
            [
                (near, s + 1, chip - s - 1),
                (mid, s, chip - 8 - s),
                (back_mid, s, chip - 8 + s),
                (far, s, chip - 16 + s),
            ]
        )
    steps.append([(mid, 4, chip - 12)])
    ids = jnp.stack([i for step in steps for _, _, i in step])
    cols = 2 * ids[:, None] + jnp.stack([core, 1 - core])[None, :]
    cols = jnp.where(ids[:, None] >= 0, cols, -1)
    hot = cols[:, None, :, None] == jnp.arange(64, dtype=jnp.int32)[None, None, None, :]
    table = jnp.sum(jnp.where(hot, lists[None, :, None, :], 0.0), axis=-1)
    table = table.astype(jnp.int32).reshape(ids.shape[0], 4)

    core1 = core.reshape(1)
    state = None
    at = 0
    for n, step in enumerate(steps):
        flags = table[at : at + len(step)]
        at += len(step)
        gates = (gate_rows, gate_other) if n == len(steps) - 1 else None
        units = [chain[k] for chain, k, _ in step]
        if n >= 1 and n < len(steps) - 1:
            if len(near) == n + 1 and n + 1 < len(NEAR_UP):
                near.append(send(near[-1], NEAR_UP[n + 1]))
            advance(n)
        state = attend_call(
            core1, flags, q, qdocs, units, state, gates, 0 if n == 0 else None
        )
        if 1 <= n < len(steps) - 2:
            far[-1], state = lax.optimization_barrier((far[-1], state))
    mine, other = state
    back = send(other, SWAP)
    return jnp.where(
        core == 0,
        jnp.concatenate([mine, back], axis=1),
        jnp.concatenate([back, mine], axis=1),
    )


def solution(mesh):
    return jax.shard_map(
        on_device,
        mesh=mesh,
        in_specs=(
            P(("dp", "cp"), None),
            P(("dp", "cp"), None),
            P(("dp", "cp"), None),
            P(("dp", "cp"), None),
            P(("dp", "cp")),
            P(("dp", "cp"), None),
        ),
        out_specs=P(("dp", "cp"), None),
        check_vma=False,
    )
```

```python
import functools
import math

import jax
import jax.numpy as jnp
from jax import lax
from jax.experimental import pallas as pl
from jax.experimental.pallas import tpu as pltpu
from jax.sharding import PartitionSpec as P

H = 16
KVH = 2
HD = 256
BLK = 128
GROUPS = H // KVH
NX, NZ = 4, 8
UNIT = 2 * BLK
META = 16
ROWS = GROUPS * UNIT
HALF = GROUPS * HD
LOG2E = 1.4426950408889634
NEG = -1e30


def pairs_of(links):
    return [
        ((ax * NZ + az) * 2 + c, (bx * NZ + bz) * 2 + c)
        for (ax, az), (bx, bz) in sorted(links)
        for c in range(2)
    ]


CHIPS = [(x, z) for x in range(NX) for z in range(NZ)]


def chain_plan(seed, source, visible, length):
    wanted = [set() for _ in range(length + 1)]
    for s in range(length, -1, -1):
        wanted[s] |= {chip for chip in CHIPS if visible(*chip, s)}
        if s:
            wanted[s - 1] |= {source(*chip) for chip in wanted[s]}
    hops = [
        pairs_of({(source(*chip), chip) for chip in wanted[s]})
        for s in range(1, length + 1)
    ]
    first, need = [], wanted[0]
    for back in seed:
        first.append(pairs_of({(back(*chip), chip) for chip in need}))
        need = {back(*chip) for chip in need}
    return first[::-1], hops


SWAP = [(i, i ^ 1) for i in range(2 * NX * NZ)]
NEAR = chain_plan(
    [],
    lambda x, z: (x, z - 1) if z else ((x - 2) % NX, NZ - 1),
    lambda x, z, s: z >= s or x >= 2,
    4,
)[1]
FAR_SEED, FAR = chain_plan(
    [lambda x, z: ((x + 1) % NX, z)] * 2,
    lambda x, z: (x, z + 1) if z < NZ - 1 else ((x + 2) % NX, 0),
    lambda x, z, s: z + s >= NZ or x >= 2,
    3,
)
MID_SEED, MID_UP = chain_plan(
    [lambda x, z: (x - 1, z)],
    lambda x, z: (x, (z - 1) % NZ),
    lambda x, z, s: x >= 1,
    3,
)
MID_DOWN = chain_plan([], lambda x, z: (x, (z + 1) % NZ), lambda x, z, s: x >= 1, 4)[1]


def attend(own_at, last, count, *refs):
    flags, core, q, qdocs = refs[:4]
    units = refs[4 : 4 + count]
    rest = list(refs[4 + count :])
    first = own_at is not None
    if not first:
        stats_in, acc_in = rest[:2]
        rest = rest[2:]
    if last:
        gate_mine, gate_other = rest[:2]
        rest = rest[2:]
        out_mine, out_other = rest[:2]
    else:
        stats_out, acc_out = rest[:2]
        rest = rest[2:]
        spot = lax.broadcasted_iota(jnp.int32, (UNIT, BLK), 1)
        stats = jnp.zeros((UNIT, BLK), jnp.float32)
    me = core[0]
    lane = lax.broadcasted_iota(jnp.int32, (1, UNIT), 1)
    biases = []
    for j in range(count):
        kd = units[j][UNIT : UNIT + META, :].astype(jnp.float32)[0:1, :]
        halves = []
        for r in range(2):
            listed = jnp.where(lane < BLK, flags[j, 2 * r], flags[j, 2 * r + 1])
            kd_r = jnp.where(listed == 1, kd, -1.0)
            qd = qdocs[r * BLK : (r + 1) * BLK, :]
            qd = jnp.concatenate([qd, qd], axis=1)
            seen = qd == kd_r
            if own_at == j:
                col = lax.broadcasted_iota(jnp.int32, (BLK, UNIT), 1)
                row = lax.broadcasted_iota(jnp.int32, (BLK, UNIT), 0)
                low = jnp.where(me == 0, col, lax.rem(col + BLK, UNIT))
                place = row + jnp.where(me == r, 0, BLK)
                seen = seen & (low <= place)
            halves.append(jnp.where(seen, 0.0, NEG))
        biases.append(jnp.concatenate(halves, axis=0))
    scale = LOG2E / math.sqrt(HD)
    for h in range(GROUPS):
        qh = q[h * UNIT : (h + 1) * UNIT, :]
        scores = []
        for j in range(count):
            s = lax.dot_general(
                qh,
                units[j][0:UNIT, :],
                (((1,), (1,)), ((), ())),
                preferred_element_type=jnp.float32,
            )
            scores.append(s * scale + biases[j])
        top = scores[0]
        for s in scores[1:]:
            top = jnp.maximum(top, s)
        top = jnp.max(top, axis=1, keepdims=True)
        if not first:
            m_old = stats_in[:, h : h + 1]
            top = jnp.maximum(m_old, top)
            alpha = jnp.exp2(m_old - top)
        total = None
        product = None
        for j in range(count):
            p = jnp.exp2(scores[j] - top)
            part = p[:, :BLK] + p[:, BLK:]
            total = part if total is None else total + part
            pv = jnp.dot(
                p.astype(jnp.bfloat16),
                units[j][UNIT + META :, :],
                preferred_element_type=jnp.float32,
            )
            product = pv if product is None else product + pv
        total = jnp.sum(total, axis=1, keepdims=True)
        if not first:
            total = total + alpha * stats_in[:, GROUPS + h : GROUPS + h + 1]
            product = product + alpha * acc_in[h]
        if last:
            inv = 1.0 / total
            att = product * inv
            base = pl.multiple_of(me * HALF + h * HD, HD)
            g = gate_mine[:, pl.ds(base, HD)].astype(jnp.float32)
            out_mine[:, h * HD : (h + 1) * HD] = (
                att[:BLK] * jax.nn.sigmoid(g)
            ).astype(jnp.bfloat16)
            g = gate_other[:, h * HD : (h + 1) * HD].astype(jnp.float32)
            out_other[:, h * HD : (h + 1) * HD] = (
                att[BLK:] * jax.nn.sigmoid(g)
            ).astype(jnp.bfloat16)
        else:
            stats = jnp.where(spot == h, top, stats)
            stats = jnp.where(spot == GROUPS + h, total, stats)
            acc_out[h] = product
    if not last:
        stats_out[...] = stats


def attend_call(core, flags, q, qdocs, units, state=None, gates=None, own_at=None):
    count = len(units)
    last = gates is not None
    smem = pl.BlockSpec(memory_space=pltpu.SMEM)
    vmem = pl.BlockSpec(memory_space=pltpu.VMEM)
    args = [flags, core, q, qdocs, *units]
    aliases = {}
    if state is not None:
        if not last:
            aliases = {len(args) + i: i for i in range(2)}
        args += list(state)
    if last:
        args += list(gates)
        shapes = [jax.ShapeDtypeStruct((BLK, HALF), jnp.bfloat16)] * 2
    else:
        shapes = [
            jax.ShapeDtypeStruct((UNIT, BLK), jnp.float32),
            jax.ShapeDtypeStruct((GROUPS, UNIT, HD), jnp.float32),
        ]
    specs = [smem, smem] + [vmem] * (len(args) - 2)
    return pl.pallas_call(
        functools.partial(attend, own_at, last, count),
        out_shape=shapes,
        in_specs=specs,
        out_specs=[vmem] * len(shapes),
        input_output_aliases=aliases,
        compiler_params=pltpu.CompilerParams(vmem_limit_bytes=16 << 20),
        cost_estimate=pl.CostEstimate(
            flops=4 * ROWS * UNIT * HD * count,
            bytes_accessed=count * 270000 + 9000000,
            transcendentals=ROWS * UNIT * count,
        ),
    )(*args)


def on_device(query_rows, key_rows, value_rows, gate_rows, doc_ids, block_lists):
    place = lax.axis_index("cp")
    core = lax.rem(place, 2)
    chip = place // 2
    x, z = chip // NZ, lax.rem(chip, NZ)

    def send(value, pairs):
        return lax.ppermute(value, "cp", pairs)

    def take(rows, which, width):
        return lax.dynamic_slice_in_dim(rows, which * width, width, 1)

    docs_row = doc_ids.astype(jnp.bfloat16).reshape(1, BLK)
    lists_row = jnp.pad(
        block_lists.astype(jnp.bfloat16), ((0, 0), (0, BLK - block_lists.shape[1]))
    )
    notes = jnp.concatenate(
        [docs_row, lists_row, jnp.zeros((META - 2, BLK), jnp.bfloat16)], axis=0
    )
    notes_wide = jnp.concatenate([notes, jnp.zeros_like(notes)], axis=1)
    parcel = jnp.concatenate(
        [take(key_rows, 1 - core, HD), take(value_rows, 1 - core, HD), notes_wide], axis=0
    )
    got = send(parcel, SWAP)
    unit = jnp.concatenate(
        [
            take(key_rows, core, HD),
            got[:BLK],
            jnp.concatenate([notes, got[2 * BLK :, :BLK]], axis=1),
            take(value_rows, core, HD),
            got[BLK : 2 * BLK],
        ],
        axis=0,
    )
    near, mid, far = [unit], [send(unit, MID_SEED[0])], []
    near.append(send(unit, NEAR[0]))
    relay = send(unit, FAR_SEED[0])
    far.append(send(relay, FAR_SEED[1]))
    back_mid = [mid[0]]
    rings = (near, NEAR), (mid, MID_UP), (back_mid, MID_DOWN), (far, FAR)

    q_other = send(take(query_rows, 1 - core, HALF), SWAP)
    gate_other = send(take(gate_rows, 1 - core, HALF), SWAP)
    q = jnp.concatenate([take(query_rows, core, HALF), q_other], axis=0)
    q = q.reshape(UNIT, GROUPS, HD).transpose(1, 0, 2).reshape(ROWS, HD)
    meta = unit[UNIT : UNIT + 2].astype(jnp.float32)
    qdocs = jnp.broadcast_to(meta[0][:, None], (UNIT, BLK))
    lists = jnp.stack([meta[1, :64], meta[1, BLK : BLK + 64]])

    def near_id(s):
        return jnp.where(z >= s, chip - s, jnp.where(x >= 2, chip - s - NZ, -1))

    def far_id(s):
        return jnp.where(
            z + s < NZ, jnp.where(x >= 2, chip - 2 * NZ + s, -1), chip + s - NZ
        )

    def mid_id(s):
        return jnp.where(x >= 1, (x - 1) * NZ + lax.rem(z + s + NZ, NZ), -1)

    steps = [
        [(near, 0, chip)],
        [(near, 1, near_id(1)), (mid, 0, mid_id(0))],
        [(near, 2, near_id(2)), (mid, 1, mid_id(-1)), (back_mid, 1, mid_id(1)), (far, 0, far_id(0))],
        [(near, 3, near_id(3)), (mid, 2, mid_id(-2)), (back_mid, 2, mid_id(2)), (far, 1, far_id(1))],
        [(near, 4, near_id(4)), (mid, 3, mid_id(-3)), (back_mid, 3, mid_id(3)), (far, 2, far_id(2))],
        [(back_mid, 4, mid_id(4)), (far, 3, far_id(3))],
    ]
    ids = jnp.stack([i for step in steps for _, _, i in step])
    cols = 2 * ids[:, None] + jnp.stack([core, 1 - core])[None, :]
    cols = jnp.where(ids[:, None] >= 0, cols, -1)
    hot = cols[:, None, :, None] == jnp.arange(64, dtype=jnp.int32)[None, None, None, :]
    table = jnp.sum(jnp.where(hot, lists[None, :, None, :], 0.0), axis=-1)
    table = table.astype(jnp.int32).reshape(ids.shape[0], 4)

    core1 = core.reshape(1)
    state = None
    at = 0
    for n, step in enumerate(steps):
        flags = table[at : at + len(step)]
        at += len(step)
        gates = (gate_rows, gate_other) if n == len(steps) - 1 else None
        for chain, hops in rings:
            due = n - 1 if chain is far else n + 1 if chain is near else n
            if len(chain) == due and due <= len(hops):
                chain.append(send(chain[-1], hops[due - 1]))
        units = [chain[k] for chain, k, _ in step]
        state = attend_call(
            core1, flags, q, qdocs, units, state, gates, 0 if n == 0 else None
        )
        if 1 <= n < len(steps) - 2:
            back_mid[-1], state = lax.optimization_barrier((back_mid[-1], state))
    mine, other = state
    back = send(other, SWAP)
    return jnp.where(
        core == 0,
        jnp.concatenate([mine, back], axis=1),
        jnp.concatenate([back, mine], axis=1),
    )


def solution(mesh):
    return jax.shard_map(
        on_device,
        mesh=mesh,
        in_specs=(
            P(("dp", "cp"), None),
            P(("dp", "cp"), None),
            P(("dp", "cp"), None),
            P(("dp", "cp"), None),
            P(("dp", "cp")),
            P(("dp", "cp"), None),
        ),
        out_specs=P(("dp", "cp"), None),
        check_vma=False,
    )
```

```python
import functools
import math

import jax
import jax.numpy as jnp
from jax import lax
from jax.experimental import pallas as pl
from jax.experimental.pallas import tpu as pltpu
from jax.sharding import PartitionSpec as P

H = 16
KVH = 2
HD = 256
BLK = 128
GROUPS = H // KVH
NX, NZ = 4, 8
UNIT = 2 * BLK
META = 16
ROWS = GROUPS * UNIT
HALF = GROUPS * HD
LOG2E = 1.4426950408889634
NEG = -1e30


def pairs_of(links):
    return [
        ((ax * NZ + az) * 2 + c, (bx * NZ + bz) * 2 + c)
        for (ax, az), (bx, bz) in sorted(links)
        for c in range(2)
    ]


CHIPS = [(x, z) for x in range(NX) for z in range(NZ)]


def chain_plan(seed, source, visible, length):
    wanted = [set() for _ in range(length + 1)]
    for s in range(length, -1, -1):
        wanted[s] |= {chip for chip in CHIPS if visible(*chip, s)}
        if s:
            wanted[s - 1] |= {source(*chip) for chip in wanted[s]}
    hops = [
        pairs_of({(source(*chip), chip) for chip in wanted[s]})
        for s in range(1, length + 1)
    ]
    first, need = [], wanted[0]
    for back in seed:
        first.append(pairs_of({(back(*chip), chip) for chip in need}))
        need = {back(*chip) for chip in need}
    return first[::-1], hops


SWAP = [(i, i ^ 1) for i in range(2 * NX * NZ)]
NEAR = chain_plan([], lambda x, z: (x, z - 1), lambda x, z, s: z >= s, 4)[1]
FAR_SEED, FAR = chain_plan(
    [lambda x, z: ((x + 1) % NX, z)] * 2,
    lambda x, z: (x, z + 1),
    lambda x, z, s: x >= 2 and z + s < NZ,
    3,
)
MID_SEED, MID_UP = chain_plan(
    [lambda x, z: ((x - 1) % NX, z)],
    lambda x, z: (x, (z - 1) % NZ),
    lambda x, z, s: x >= 1,
    3,
)
MID_SEED_DOWN, MID_DOWN = chain_plan(
    [lambda x, z: ((x - 1) % NX, z)],
    lambda x, z: (x, (z + 1) % NZ),
    lambda x, z, s: x >= 1 or (z + s >= NZ and s < 4),
    4,
)
MID_SEED = sorted(set(MID_SEED[0]) | set(MID_SEED_DOWN[0]))
SIDE_NEAR = [
    pairs_of({((x - 1, z), (x, z)) for x, z in CHIPS if x >= 2 and z < s})
    for s in range(1, 5)
]
SIDE_FAR = [
    pairs_of({(((x + 1) % NX, z), (x, z)) for x, z in CHIPS if z + s >= NZ})
    for s in range(1, 4)
]


def attend(own_at, last, paired, *refs):
    flags, core, q, qdocs = refs[:4]
    rest = list(refs[4:])
    units = []
    for j, two in enumerate(paired):
        if two:
            other = flags[j, 4] == 1
            units.append(jnp.where(other, rest[1][...], rest[0][...]))
        else:
            units.append(rest[0])
        rest = rest[2 if two else 1 :]
    count = len(paired)
    first = own_at is not None
    if not first:
        m_in, l_in, acc_in = rest[:3]
        rest = rest[3:]
    if last:
        gate_mine, gate_other = rest[:2]
        rest = rest[2:]
        out_mine, out_other = rest[:2]
    else:
        m_out, l_out, acc_out = rest[:3]
        rest = rest[3:]
    me = core[0]
    lane = lax.broadcasted_iota(jnp.int32, (1, UNIT), 1)
    biases = []
    for j in range(count):
        kd = units[j][UNIT : UNIT + META, :].astype(jnp.float32)[0:1, :]
        halves = []
        for r in range(2):
            listed = jnp.where(lane < BLK, flags[j, 2 * r], flags[j, 2 * r + 1])
            kd_r = jnp.where(listed == 1, kd, -1.0)
            qd = qdocs[r * BLK : (r + 1) * BLK, :]
            qd = jnp.concatenate([qd, qd], axis=1)
            seen = qd == kd_r
            if own_at == j:
                col = lax.broadcasted_iota(jnp.int32, (BLK, UNIT), 1)
                row = lax.broadcasted_iota(jnp.int32, (BLK, UNIT), 0)
                low = jnp.where(me == 0, col, lax.rem(col + BLK, UNIT))
                place = row + jnp.where(me == r, 0, BLK)
                seen = seen & (low <= place)
            halves.append(jnp.where(seen, 0.0, NEG))
        biases.append(jnp.concatenate(halves, axis=0))
    scale = LOG2E / math.sqrt(HD)
    for h in range(GROUPS):
        qh = q[h * UNIT : (h + 1) * UNIT, :]
        scores = []
        for j in range(count):
            s = lax.dot_general(
                qh,
                units[j][0:UNIT, :],
                (((1,), (1,)), ((), ())),
                preferred_element_type=jnp.float32,
            )
            scores.append(s * scale + biases[j])
        top = scores[0]
        for s in scores[1:]:
            top = jnp.maximum(top, s)
        top = jnp.max(top, axis=1, keepdims=True)
        if first:
            m_new = jnp.broadcast_to(top, (UNIT, BLK))
        else:
            m_old = m_in[h]
            m_new = jnp.maximum(m_old, top)
            alpha = jnp.exp2(m_old - m_new)
        m_wide = jnp.concatenate([m_new, m_new], axis=1)
        total = None
        product = None
        for j in range(count):
            p = jnp.exp2(scores[j] - m_wide)
            part = p[:, :BLK] + p[:, BLK:]
            total = part if total is None else total + part
            pv = jnp.dot(
                p.astype(jnp.bfloat16),
                units[j][UNIT + META :, :],
                preferred_element_type=jnp.float32,
            )
            product = pv if product is None else product + pv
        if not first:
            total = total + alpha * l_in[h]
            wide = jnp.concatenate([alpha, alpha], axis=1)
            product = product + wide * acc_in[h]
        if last:
            inv = 1.0 / jnp.sum(total, axis=1, keepdims=True)
            att = product * inv
            base = pl.multiple_of(me * HALF + h * HD, HD)
            g = gate_mine[:, pl.ds(base, HD)].astype(jnp.float32)
            out_mine[:, h * HD : (h + 1) * HD] = (
                att[:BLK] * jax.nn.sigmoid(g)
            ).astype(jnp.bfloat16)
            g = gate_other[:, h * HD : (h + 1) * HD].astype(jnp.float32)
            out_other[:, h * HD : (h + 1) * HD] = (
                att[BLK:] * jax.nn.sigmoid(g)
            ).astype(jnp.bfloat16)
        else:
            m_out[h] = m_new
            l_out[h] = total
            acc_out[h] = product


def attend_call(core, flags, q, qdocs, units, state=None, gates=None, own_at=None):
    count = len(units)
    paired = tuple(len(u) == 2 for u in units)
    units = [v for u in units for v in u]
    last = gates is not None
    smem = pl.BlockSpec(memory_space=pltpu.SMEM)
    vmem = pl.BlockSpec(memory_space=pltpu.VMEM)
    args = [flags, core, q, qdocs, *units]
    aliases = {}
    if state is not None:
        if not last:
            aliases = {len(args) + i: i for i in range(3)}
        args += list(state)
    if last:
        args += list(gates)
        shapes = [jax.ShapeDtypeStruct((BLK, HALF), jnp.bfloat16)] * 2
    else:
        shapes = [
            jax.ShapeDtypeStruct((GROUPS, UNIT, BLK), jnp.float32),
            jax.ShapeDtypeStruct((GROUPS, UNIT, BLK), jnp.float32),
            jax.ShapeDtypeStruct((GROUPS, UNIT, HD), jnp.float32),
        ]
    specs = [smem, smem] + [vmem] * (len(args) - 2)
    return pl.pallas_call(
        functools.partial(attend, own_at, last, paired),
        out_shape=shapes,
        in_specs=specs,
        out_specs=[vmem] * len(shapes),
        input_output_aliases=aliases,
        compiler_params=pltpu.CompilerParams(vmem_limit_bytes=24 << 20),
        cost_estimate=pl.CostEstimate(
            flops=4 * ROWS * UNIT * HD * count,
            bytes_accessed=count * 270000 + 9000000,
            transcendentals=ROWS * UNIT * count,
        ),
    )(*args)


def on_device(query_rows, key_rows, value_rows, gate_rows, doc_ids, block_lists):
    place = lax.axis_index("cp")
    core = lax.rem(place, 2)
    chip = place // 2
    x, z = chip // NZ, lax.rem(chip, NZ)

    def send(value, pairs):
        return lax.ppermute(value, "cp", pairs)

    def take(rows, which, width):
        return lax.dynamic_slice_in_dim(rows, which * width, width, 1)

    docs_row = doc_ids.astype(jnp.bfloat16).reshape(1, BLK)
    lists_row = jnp.pad(
        block_lists.astype(jnp.bfloat16), ((0, 0), (0, BLK - block_lists.shape[1]))
    )
    notes = jnp.concatenate(
        [docs_row, lists_row, jnp.zeros((META - 2, BLK), jnp.bfloat16)], axis=0
    )
    notes_wide = jnp.concatenate([notes, jnp.zeros_like(notes)], axis=1)
    parcel = jnp.concatenate(
        [take(key_rows, 1 - core, HD), take(value_rows, 1 - core, HD), notes_wide], axis=0
    )
    got = send(parcel, SWAP)
    unit = jnp.concatenate(
        [
            take(key_rows, core, HD),
            got[:BLK],
            jnp.concatenate([notes, got[2 * BLK :, :BLK]], axis=1),
            take(value_rows, core, HD),
            got[BLK : 2 * BLK],
        ],
        axis=0,
    )
    near, mid, far = [unit], [send(unit, MID_SEED)], []
    near.append(send(unit, NEAR[0]))
    relay = send(unit, FAR_SEED[0])
    far.append(send(relay, FAR_SEED[1]))
    low, high = [mid[0]], [mid[0]]
    side_near, side_far = [None], [None]
    for s in range(4):
        high.append(send(high[-1], MID_DOWN[s]))
        if s < 3:
            low.append(send(low[-1], MID_UP[s]))
            near.append(send(near[-1], NEAR[s + 1]))
            far.append(send(far[-1], FAR[s]))
            side_near.append(send(low[-1], SIDE_NEAR[s]))
            side_far.append(send(high[-1], SIDE_FAR[s]))
        else:
            side_near.append(send(high[-1], SIDE_NEAR[s]))

    q_other = send(take(query_rows, 1 - core, HALF), SWAP)
    gate_other = send(take(gate_rows, 1 - core, HALF), SWAP)
    q = jnp.concatenate([take(query_rows, core, HALF), q_other], axis=0)
    q = q.reshape(UNIT, GROUPS, HD).transpose(1, 0, 2).reshape(ROWS, HD)
    meta = unit[UNIT : UNIT + 2].astype(jnp.float32)
    qdocs = jnp.broadcast_to(meta[0][:, None], (UNIT, BLK))
    lists = jnp.stack([meta[1, :64], meta[1, BLK : BLK + 64]])

    def mid_unit(s):
        unit_id = jnp.where(x >= 1, (x - 1) * NZ + lax.rem(z + s + NZ, NZ), -1)
        return ((low[-s] if s <= 0 else high[s]),), unit_id, jnp.int32(0)

    def near_unit(s):
        over = z < s
        unit_id = jnp.where(over, jnp.where(x >= 2, chip - s - NZ, -1), chip - s)
        return (near[s], side_near[s]), unit_id, over.astype(jnp.int32)

    def far_unit(s):
        if s == 0:
            return (far[0],), jnp.where(x >= 2, chip - 2 * NZ, -1), jnp.int32(0)
        over = z + s >= NZ
        unit_id = jnp.where(
            over, chip + s - NZ, jnp.where(x >= 2, chip - 2 * NZ + s, -1)
        )
        return (far[s], side_far[s]), unit_id, over.astype(jnp.int32)

    groups = [
        [((unit,), chip, jnp.int32(0))],
        [mid_unit(0), mid_unit(-1), mid_unit(1), far_unit(0)],
        [mid_unit(-2), mid_unit(2), near_unit(1), far_unit(1)],
        [mid_unit(-3), mid_unit(3), near_unit(2), far_unit(2)],
        [mid_unit(4), near_unit(3), far_unit(3), near_unit(4)],
    ]
    ids = jnp.stack([i for group in groups for _, i, _ in group])
    cols = 2 * ids[:, None] + jnp.stack([core, 1 - core])[None, :]
    cols = jnp.where(ids[:, None] >= 0, cols, -1)
    hot = cols[:, None, :, None] == jnp.arange(64, dtype=jnp.int32)[None, None, None, :]
    table = jnp.sum(jnp.where(hot, lists[None, :, None, :], 0.0), axis=-1)
    table = table.astype(jnp.int32).reshape(ids.shape[0], 4)
    picks = jnp.stack([k for group in groups for _, _, k in group])
    table = jnp.concatenate([table, picks[:, None]], axis=1)

    core1 = core.reshape(1)
    state = None
    at = 0
    for n, group in enumerate(groups):
        flags = table[at : at + len(group)]
        at += len(group)
        gates = (gate_rows, gate_other) if n == len(groups) - 1 else None
        state = attend_call(
            core1, flags, q, qdocs, [u for u, _, _ in group], state, gates, 0 if n == 0 else None
        )
    mine, other = state
    back = send(other, SWAP)
    return jnp.where(
        core == 0,
        jnp.concatenate([mine, back], axis=1),
        jnp.concatenate([back, mine], axis=1),
    )


def solution(mesh):
    return jax.shard_map(
        on_device,
        mesh=mesh,
        in_specs=(
            P(("dp", "cp"), None),
            P(("dp", "cp"), None),
            P(("dp", "cp"), None),
            P(("dp", "cp"), None),
            P(("dp", "cp")),
            P(("dp", "cp"), None),
        ),
        out_specs=P(("dp", "cp"), None),
        check_vma=False,
    )
```

```python
import functools
import math

import jax
import jax.numpy as jnp
from jax import lax
from jax.experimental import pallas as pl
from jax.experimental.pallas import tpu as pltpu
from jax.sharding import PartitionSpec as P

H = 16
KVH = 2
HD = 256
BLK = 128
GROUPS = H // KVH
NX, NZ = 4, 8
UNIT = 2 * BLK
META = 16
WIDE = KVH * HD
LOG2E = 1.4426950408889634
NEG = -1e30


CHIPS = [(x, z) for x in range(NX) for z in range(NZ)]


def pairs_of(core, links):
    return [
        ((ax * NZ + az) * 2 + core, (bx * NZ + bz) * 2 + core)
        for (ax, az), (bx, bz) in sorted(links)
    ]


def chain_plan(seed, source, visible, length):
    wanted = [set() for _ in range(length + 1)]
    for s in range(length, -1, -1):
        wanted[s] |= {chip for chip in CHIPS if visible(*chip, s)}
        if s:
            wanted[s - 1] |= {source(*chip) for chip in wanted[s]}
    first = {(seed(*chip), chip) for chip in wanted[0]} if seed else set()
    hops = [first]
    for s in range(1, length + 1):
        hops.append({(source(*chip), chip) for chip in wanted[s]})
    return hops


NEAR = chain_plan(
    None,
    lambda x, z: (x, z - 1) if z else ((x - 2) % NX, NZ - 1),
    lambda x, z, s: z >= s or x >= 2,
    4,
)
FAR = chain_plan(
    lambda x, z: ((x + 2) % NX, z),
    lambda x, z: (x, z + 1) if z < NZ - 1 else ((x + 2) % NX, 0),
    lambda x, z, s: z + s >= NZ or x >= 2,
    3,
)
MID_UP = chain_plan(
    lambda x, z: (x - 1, z), lambda x, z: (x, (z - 1) % NZ), lambda x, z, s: x >= 1, 3
)
MID_DOWN = chain_plan(
    None, lambda x, z: (x, (z + 1) % NZ), lambda x, z, s: x >= 1, 4
)
SWAP = [(i, i ^ 1) for i in range(2 * NX * NZ)]
UP = [pairs_of(0, NEAR[s]) + pairs_of(1, MID_UP[s - 1]) for s in range(1, 5)]
SEED = pairs_of(0, FAR[0])
DOWN = [pairs_of(0, FAR[s]) + pairs_of(1, MID_DOWN[s]) for s in range(1, 4)]
LAST = pairs_of(1, MID_DOWN[4])


def attend(first, last, paired, *refs):
    flags, core, qdocs, q_mine, q_other = refs[:5]
    rest = list(refs[5:])
    units = []
    for j, two in enumerate(paired):
        if two:
            units.append(jnp.where(core[0] == 1, rest[1][...], rest[0][...]))
        else:
            units.append(rest[0])
        rest = rest[2 if two else 1 :]
    count = len(paired)
    if not first:
        m_in, l_in, acc_in = rest[:3]
        rest = rest[3:]
    spot = lax.broadcasted_iota(jnp.int32, (BLK, BLK), 1)
    if last:
        acc_out, stats_out, share_out, share_stats_out = rest[:4]
        stats = jnp.zeros((BLK, BLK), jnp.float32)
        share_stats = jnp.zeros((BLK, BLK), jnp.float32)
    else:
        m_out, l_out, acc_out = rest[:3]
    me = core[0]
    lane = lax.broadcasted_iota(jnp.int32, (1, UNIT), 1)
    biases = []
    for j in range(count):
        kd = units[j][UNIT : UNIT + META, :UNIT].astype(jnp.float32)[0:1, :]
        halves = []
        for r in range(2):
            listed = jnp.where(lane < BLK, flags[j, 2 * r], flags[j, 2 * r + 1])
            kd_r = jnp.where(listed == 1, kd, -1.0)
            qd = qdocs[r * BLK : (r + 1) * BLK, :]
            qd = jnp.concatenate([qd, qd], axis=1)
            seen = qd == kd_r
            if first and j == 0:
                col = lax.broadcasted_iota(jnp.int32, (BLK, UNIT), 1)
                row = lax.broadcasted_iota(jnp.int32, (BLK, UNIT), 0)
                low = jnp.where(me == 0, col, lax.rem(col + BLK, UNIT))
                place = row + jnp.where(me == r, 0, BLK)
                seen = seen & (low <= place)
            halves.append(jnp.where(seen, 0.0, NEG))
        biases.append(jnp.concatenate(halves, axis=0))
    scale = LOG2E / math.sqrt(HD)
    for h in range(H):
        at = slice(h * HD, (h + 1) * HD)
        kv = slice(h // GROUPS * HD, (h // GROUPS + 1) * HD)
        qh = jnp.concatenate([q_mine[:, at], q_other[:, at]], axis=0)
        scores = []
        for j in range(count):
            s = lax.dot_general(
                qh,
                units[j][0:UNIT, kv],
                (((1,), (1,)), ((), ())),
                preferred_element_type=jnp.float32,
            )
            scores.append(s * scale + biases[j])
        top = scores[0]
        for s in scores[1:]:
            top = jnp.maximum(top, s)
        top = jnp.max(top, axis=1, keepdims=True)
        if first:
            m_new = jnp.broadcast_to(top, (UNIT, BLK))
        else:
            m_old = m_in[h]
            m_new = jnp.maximum(m_old, top)
            alpha = jnp.exp2(m_old - m_new)
        m_wide = jnp.concatenate([m_new, m_new], axis=1)
        total = None
        product = None
        for j in range(count):
            p = jnp.exp2(scores[j] - m_wide)
            part = p[:, :BLK] + p[:, BLK:]
            total = part if total is None else total + part
            pv = jnp.dot(
                p.astype(jnp.bfloat16),
                units[j][UNIT + META :, kv],
                preferred_element_type=jnp.float32,
            )
            product = pv if product is None else product + pv
        if not first:
            total = total + alpha * l_in[h]
            wide = jnp.concatenate([alpha, alpha], axis=1)
            product = product + wide * acc_in[h]
        if last:
            total = jnp.sum(total, axis=1, keepdims=True)
            acc_out[h] = product[:BLK]
            share_out[h] = (product[BLK:] / total[BLK:]).astype(jnp.bfloat16)
            stats = jnp.where(spot == h, m_new[:BLK], stats)
            stats = jnp.where(spot == H + h, total[:BLK], stats)
            share_stats = jnp.where(spot == h, m_new[BLK:], share_stats)
            share_stats = jnp.where(spot == H + h, total[BLK:], share_stats)
        else:
            m_out[h] = m_new
            l_out[h] = total
            acc_out[h] = product
    if last:
        stats_out[...] = stats
        share_stats_out[...] = share_stats


def attend_call(core, flags, queries, qdocs, units, state, last):
    paired = tuple(len(u) == 2 for u in units)
    smem = pl.BlockSpec(memory_space=pltpu.SMEM)
    vmem = pl.BlockSpec(memory_space=pltpu.VMEM)
    args = [flags, core, qdocs, *queries, *[v for u in units for v in u]]
    aliases = {}
    if state is not None:
        if not last:
            aliases = {len(args) + i: i for i in range(3)}
        args += list(state)
    if last:
        shapes = [
            jax.ShapeDtypeStruct((H, BLK, HD), jnp.float32),
            jax.ShapeDtypeStruct((BLK, BLK), jnp.float32),
            jax.ShapeDtypeStruct((H, BLK, HD), jnp.bfloat16),
            jax.ShapeDtypeStruct((BLK, BLK), jnp.float32),
        ]
    else:
        shapes = [
            jax.ShapeDtypeStruct((H, UNIT, BLK), jnp.float32),
            jax.ShapeDtypeStruct((H, UNIT, BLK), jnp.float32),
            jax.ShapeDtypeStruct((H, UNIT, HD), jnp.float32),
        ]
    return pl.pallas_call(
        functools.partial(attend, state is None, last, paired),
        out_shape=shapes,
        in_specs=[smem, smem] + [vmem] * (len(args) - 2),
        out_specs=[vmem] * len(shapes),
        input_output_aliases=aliases,
        compiler_params=pltpu.CompilerParams(vmem_limit_bytes=24 << 20),
        cost_estimate=pl.CostEstimate(
            flops=12 * H * UNIT * UNIT * HD * len(units),
            bytes_accessed=len(units) * 540000 + 9000000,
            transcendentals=H * UNIT * UNIT * len(units),
        ),
    )(*args)


def combine(acc, stats, share, share_stats, gate, out):
    for h in range(H):
        at = slice(h * HD, (h + 1) * HD)
        m0, m1 = stats[:, h : h + 1], share_stats[:, h : h + 1]
        l0, l1 = stats[:, H + h : H + h + 1], share_stats[:, H + h : H + h + 1]
        top = jnp.maximum(m0, m1)
        e0 = jnp.exp2(m0 - top)
        e1 = jnp.exp2(m1 - top) * l1
        inv = 1.0 / (l0 * e0 + e1)
        att = acc[h] * (e0 * inv) + share[h].astype(jnp.float32) * (e1 * inv)
        g = gate[:, at].astype(jnp.float32)
        out[:, at] = (att * jax.nn.sigmoid(g)).astype(jnp.bfloat16)


def combine_call(*args):
    vmem = pl.BlockSpec(memory_space=pltpu.VMEM)
    return pl.pallas_call(
        combine,
        out_shape=jax.ShapeDtypeStruct((BLK, H * HD), jnp.bfloat16),
        in_specs=[vmem] * len(args),
        out_specs=vmem,
        compiler_params=pltpu.CompilerParams(vmem_limit_bytes=24 << 20),
    )(*args)


def on_device(query_rows, key_rows, value_rows, gate_rows, doc_ids, block_lists):
    place = lax.axis_index("cp")
    core = lax.rem(place, 2)
    chip = place // 2
    x, z = chip // NZ, lax.rem(chip, NZ)

    def send(value, pairs):
        return lax.ppermute(value, "cp", pairs)

    docs_row = doc_ids.astype(jnp.bfloat16).reshape(1, BLK)
    lists_row = jnp.pad(
        block_lists.astype(jnp.bfloat16), ((0, 0), (0, BLK - block_lists.shape[1]))
    )
    notes = jnp.concatenate(
        [docs_row, lists_row, jnp.zeros((META - 2, BLK), jnp.bfloat16)], axis=0
    )
    notes_wide = jnp.pad(notes, ((0, 0), (0, WIDE - BLK)))
    parcel = jnp.concatenate([key_rows, value_rows, notes_wide], axis=0)
    got = send(parcel, SWAP)
    unit = jnp.concatenate(
        [
            key_rows,
            got[:BLK],
            jnp.concatenate(
                [notes, got[2 * BLK :, :BLK], jnp.zeros((META, WIDE - UNIT), jnp.bfloat16)],
                axis=1,
            ),
            value_rows,
            got[BLK : 2 * BLK],
        ],
        axis=0,
    )
    query_rows, _ = lax.optimization_barrier((query_rows, parcel))
    queries = (query_rows, send(query_rows, SWAP))

    up = [send(unit, UP[0])]
    seed = send(unit, SEED)
    down = [jnp.where(core == 0, seed, up[0])]
    for s in range(3):
        up.append(send(up[-1], UP[s + 1]))
        down.append(send(down[-1], DOWN[s]))
    end = send(down[-1], LAST)

    meta = unit[UNIT : UNIT + 2, :UNIT].astype(jnp.float32)
    qdocs = jnp.broadcast_to(meta[0][:, None], (UNIT, BLK))
    lists = jnp.stack([meta[1, :64], meta[1, BLK : BLK + 64]])

    def near_id(s):
        return jnp.where(z >= s, chip - s, jnp.where(x >= 2, chip - s - NZ, -1))

    def far_id(s):
        return jnp.where(
            z + s < NZ, jnp.where(x >= 2, chip - 2 * NZ + s, -1), chip + s - NZ
        )

    def mid_id(s):
        return jnp.where(x >= 1, (x - 1) * NZ + lax.rem(z + s + NZ, NZ), -1)

    groups = [
        [((unit,), chip, -1), ((up[0],), near_id(1), mid_id(0))],
        [((up[1],), near_id(2), mid_id(-1)), ((down[1],), far_id(1), mid_id(1))],
        [((up[2],), near_id(3), mid_id(-2)), ((down[2],), far_id(2), mid_id(2))],
        [((up[3],), near_id(4), mid_id(-3)), ((down[3],), far_id(3), mid_id(3))],
        [((seed, end), far_id(0), mid_id(4))],
    ]
    ids = jnp.stack([jnp.where(core == 0, a, b) for group in groups for _, a, b in group])
    cols = 2 * ids[:, None] + jnp.stack([core, 1 - core])[None, :]
    cols = jnp.where(ids[:, None] >= 0, cols, -1)
    hot = cols[:, None, :, None] == jnp.arange(64, dtype=jnp.int32)[None, None, None, :]
    table = jnp.sum(jnp.where(hot, lists[None, :, None, :], 0.0), axis=-1)
    table = table.astype(jnp.int32).reshape(ids.shape[0], 4)

    core1 = core.reshape(1)
    state = None
    at = 0
    for n, group in enumerate(groups):
        flags = table[at : at + len(group)]
        at += len(group)
        state = attend_call(
            core1, flags, queries, qdocs, [g[0] for g in group], state, n == len(groups) - 1
        )
    acc, stats, share, share_stats = state
    return combine_call(acc, stats, send(share, SWAP), send(share_stats, SWAP), gate_rows)


def solution(mesh):
    return jax.shard_map(
        on_device,
        mesh=mesh,
        in_specs=(
            P(("dp", "cp"), None),
            P(("dp", "cp"), None),
            P(("dp", "cp"), None),
            P(("dp", "cp"), None),
            P(("dp", "cp")),
            P(("dp", "cp"), None),
        ),
        out_specs=P(("dp", "cp"), None),
        check_vma=False,
    )
```

```python
import functools
import math

import jax
import jax.numpy as jnp
from jax import lax
from jax.experimental import pallas as pl
from jax.experimental.pallas import tpu as pltpu
from jax.sharding import PartitionSpec as P

H = 16
KVH = 2
HD = 256
BLK = 128
GROUPS = H // KVH
NX, NZ = 4, 8
UNIT = 2 * BLK
META = 16
WIDE = KVH * HD
LOG2E = 1.4426950408889634
NEG = -1e30


CHIPS = [(x, z) for x in range(NX) for z in range(NZ)]


def pairs_of(core, links):
    return [
        ((ax * NZ + az) * 2 + core, (bx * NZ + bz) * 2 + core)
        for (ax, az), (bx, bz) in sorted(links)
    ]


def chain_plan(seed, source, visible, length):
    wanted = [set() for _ in range(length + 1)]
    for s in range(length, -1, -1):
        wanted[s] |= {chip for chip in CHIPS if visible(*chip, s)}
        if s:
            wanted[s - 1] |= {source(*chip) for chip in wanted[s]}
    first = {(seed(*chip), chip) for chip in wanted[0]} if seed else set()
    hops = [first]
    for s in range(1, length + 1):
        hops.append({(source(*chip), chip) for chip in wanted[s]})
    return hops


NEAR = chain_plan(
    None,
    lambda x, z: (x, z - 1) if z else ((x - 2) % NX, NZ - 1),
    lambda x, z, s: z >= s or x >= 2,
    4,
)
FAR = chain_plan(
    lambda x, z: ((x + 2) % NX, z),
    lambda x, z: (x, z + 1) if z < NZ - 1 else ((x + 2) % NX, 0),
    lambda x, z, s: z + s >= NZ or x >= 2,
    3,
)
MID_UP = chain_plan(
    lambda x, z: (x - 1, z), lambda x, z: (x, (z - 1) % NZ), lambda x, z, s: x >= 1, 3
)
MID_DOWN = chain_plan(
    None, lambda x, z: (x, (z + 1) % NZ), lambda x, z, s: x >= 1, 4
)
SWAP = [(i, i ^ 1) for i in range(2 * NX * NZ)]
UP = [pairs_of(0, NEAR[s]) + pairs_of(1, MID_UP[s - 1]) for s in range(1, 5)]
SEED = pairs_of(0, FAR[0])
LEAD = pairs_of(1, MID_DOWN[1])
DOWN = [pairs_of(0, FAR[s]) + pairs_of(1, MID_DOWN[s + 1]) for s in range(1, 4)]


def attend(first, last, paired, *refs):
    flags, core, qdocs, q_mine, q_other = refs[:5]
    rest = list(refs[5:])
    units = []
    for j, two in enumerate(paired):
        if two:
            units.append(jnp.where(core[0] == 1, rest[1][...], rest[0][...]))
        else:
            units.append(rest[0])
        rest = rest[2 if two else 1 :]
    count = len(paired)
    if not first:
        m_in, l_in, acc_in = rest[:3]
        rest = rest[3:]
    spot = lax.broadcasted_iota(jnp.int32, (BLK, BLK), 1)
    if last:
        acc_out, stats_out, share_out, share_stats_out = rest[:4]
        stats = jnp.zeros((BLK, BLK), jnp.float32)
        share_stats = jnp.zeros((BLK, BLK), jnp.float32)
    else:
        m_out, l_out, acc_out = rest[:3]
    me = core[0]
    lane = lax.broadcasted_iota(jnp.int32, (1, UNIT), 1)
    biases = []
    for j in range(count):
        kd = units[j][UNIT : UNIT + META, :UNIT].astype(jnp.float32)[0:1, :]
        halves = []
        for r in range(2):
            listed = jnp.where(lane < BLK, flags[j, 2 * r], flags[j, 2 * r + 1])
            kd_r = jnp.where(listed == 1, kd, -1.0)
            qd = qdocs[r * BLK : (r + 1) * BLK, :]
            qd = jnp.concatenate([qd, qd], axis=1)
            seen = qd == kd_r
            if first and j == 0:
                col = lax.broadcasted_iota(jnp.int32, (BLK, UNIT), 1)
                row = lax.broadcasted_iota(jnp.int32, (BLK, UNIT), 0)
                low = jnp.where(me == 0, col, lax.rem(col + BLK, UNIT))
                place = row + jnp.where(me == r, 0, BLK)
                seen = seen & (low <= place)
            halves.append(jnp.where(seen, 0.0, NEG))
        biases.append(jnp.concatenate(halves, axis=0))
    scale = LOG2E / math.sqrt(HD)
    for h in range(H):
        at = slice(h * HD, (h + 1) * HD)
        kv = slice(h // GROUPS * HD, (h // GROUPS + 1) * HD)
        qh = jnp.concatenate([q_mine[:, at], q_other[:, at]], axis=0)
        scores = []
        for j in range(count):
            s = lax.dot_general(
                qh,
                units[j][0:UNIT, kv],
                (((1,), (1,)), ((), ())),
                preferred_element_type=jnp.float32,
            )
            scores.append(s * scale + biases[j])
        top = scores[0]
        for s in scores[1:]:
            top = jnp.maximum(top, s)
        top = jnp.max(top, axis=1, keepdims=True)
        if first:
            m_new = jnp.broadcast_to(top, (UNIT, BLK))
        else:
            m_old = m_in[h]
            m_new = jnp.maximum(m_old, top)
            alpha = jnp.exp2(m_old - m_new)
        m_wide = jnp.concatenate([m_new, m_new], axis=1)
        total = None
        product = None
        for j in range(count):
            p = jnp.exp2(scores[j] - m_wide)
            part = p[:, :BLK] + p[:, BLK:]
            total = part if total is None else total + part
            pv = jnp.dot(
                p.astype(jnp.bfloat16),
                units[j][UNIT + META :, kv],
                preferred_element_type=jnp.float32,
            )
            product = pv if product is None else product + pv
        if not first:
            total = total + alpha * l_in[h]
            wide = jnp.concatenate([alpha, alpha], axis=1)
            product = product + wide * acc_in[h]
        if last:
            total = jnp.sum(total, axis=1, keepdims=True)
            acc_out[h] = product[:BLK]
            share_out[h] = (product[BLK:] / total[BLK:]).astype(jnp.bfloat16)
            stats = jnp.where(spot == h, m_new[:BLK], stats)
            stats = jnp.where(spot == H + h, total[:BLK], stats)
            share_stats = jnp.where(spot == h, m_new[BLK:], share_stats)
            share_stats = jnp.where(spot == H + h, total[BLK:], share_stats)
        else:
            m_out[h] = m_new
            l_out[h] = total
            acc_out[h] = product
    if last:
        stats_out[...] = stats
        share_stats_out[...] = share_stats


def attend_call(core, flags, queries, qdocs, units, state, last):
    paired = tuple(len(u) == 2 for u in units)
    smem = pl.BlockSpec(memory_space=pltpu.SMEM)
    vmem = pl.BlockSpec(memory_space=pltpu.VMEM)
    args = [flags, core, qdocs, *queries, *[v for u in units for v in u]]
    aliases = {}
    if state is not None:
        if not last:
            aliases = {len(args) + i: i for i in range(3)}
        args += list(state)
    if last:
        shapes = [
            jax.ShapeDtypeStruct((H, BLK, HD), jnp.float32),
            jax.ShapeDtypeStruct((BLK, BLK), jnp.float32),
            jax.ShapeDtypeStruct((H, BLK, HD), jnp.bfloat16),
            jax.ShapeDtypeStruct((BLK, BLK), jnp.float32),
        ]
    else:
        shapes = [
            jax.ShapeDtypeStruct((H, UNIT, BLK), jnp.float32),
            jax.ShapeDtypeStruct((H, UNIT, BLK), jnp.float32),
            jax.ShapeDtypeStruct((H, UNIT, HD), jnp.float32),
        ]
    return pl.pallas_call(
        functools.partial(attend, state is None, last, paired),
        out_shape=shapes,
        in_specs=[smem, smem] + [vmem] * (len(args) - 2),
        out_specs=[vmem] * len(shapes),
        input_output_aliases=aliases,
        compiler_params=pltpu.CompilerParams(vmem_limit_bytes=24 << 20),
        cost_estimate=pl.CostEstimate(
            flops=12 * H * UNIT * UNIT * HD * len(units),
            bytes_accessed=len(units) * 540000 + 9000000,
            transcendentals=H * UNIT * UNIT * len(units),
        ),
    )(*args)


def gate_sigmoid(gate, out):
    for h in range(H):
        at = slice(h * HD, (h + 1) * HD)
        out[:, at] = jax.nn.sigmoid(gate[:, at].astype(jnp.float32))


def sigmoid_call(gate_rows):
    vmem = pl.BlockSpec(memory_space=pltpu.VMEM)
    return pl.pallas_call(
        gate_sigmoid,
        out_shape=jax.ShapeDtypeStruct(gate_rows.shape, jnp.float32),
        in_specs=[vmem],
        out_specs=vmem,
        cost_estimate=pl.CostEstimate(
            flops=2000000000, bytes_accessed=3000000, transcendentals=1000000
        ),
    )(gate_rows)


def combine(acc, stats, share, share_stats, sigmoid, out):
    m0, m1 = stats[...], share_stats[...]
    l0, l1 = (pltpu.roll(v, BLK - H, 1) for v in (m0, m1))
    top = jnp.maximum(m0, m1)
    e0 = jnp.exp2(m0 - top)
    e1 = jnp.exp2(m1 - top) * l1
    inv = 1.0 / (l0 * e0 + e1)
    w0, w1 = e0 * inv, e1 * inv
    for h in range(H):
        at = slice(h * HD, (h + 1) * HD)
        att = acc[h] * w0[:, h : h + 1] + share[h].astype(jnp.float32) * w1[:, h : h + 1]
        out[:, at] = (att * sigmoid[:, at]).astype(jnp.bfloat16)


def combine_call(*args):
    vmem = pl.BlockSpec(memory_space=pltpu.VMEM)
    return pl.pallas_call(
        combine,
        out_shape=jax.ShapeDtypeStruct((BLK, H * HD), jnp.bfloat16),
        in_specs=[vmem] * len(args),
        out_specs=vmem,
        compiler_params=pltpu.CompilerParams(vmem_limit_bytes=24 << 20),
    )(*args)


def on_device(query_rows, key_rows, value_rows, gate_rows, doc_ids, block_lists):
    place = lax.axis_index("cp")
    core = lax.rem(place, 2)
    chip = place // 2
    x, z = chip // NZ, lax.rem(chip, NZ)

    def send(value, pairs):
        return lax.ppermute(value, "cp", pairs)

    docs_row = doc_ids.astype(jnp.bfloat16).reshape(1, BLK)
    lists_row = jnp.pad(
        block_lists.astype(jnp.bfloat16), ((0, 0), (0, BLK - block_lists.shape[1]))
    )
    notes = jnp.concatenate(
        [docs_row, lists_row, jnp.zeros((META - 2, BLK), jnp.bfloat16)], axis=0
    )
    notes_wide = jnp.pad(notes, ((0, 0), (0, WIDE - BLK)))
    parcel = jnp.concatenate([key_rows, value_rows, notes_wide], axis=0)
    got = send(parcel, SWAP)
    unit = jnp.concatenate(
        [
            key_rows,
            got[:BLK],
            jnp.concatenate(
                [notes, got[2 * BLK :, :BLK], jnp.zeros((META, WIDE - UNIT), jnp.bfloat16)],
                axis=1,
            ),
            value_rows,
            got[BLK : 2 * BLK],
        ],
        axis=0,
    )
    query_rows, _ = lax.optimization_barrier((query_rows, parcel))
    queries = (query_rows, send(query_rows, SWAP))

    up = [send(unit, UP[0])]
    seed = send(unit, SEED)
    up.append(send(up[0], UP[1]))
    lead = send(up[0], LEAD)
    sigmoid = sigmoid_call(gate_rows)

    meta = unit[UNIT : UNIT + 2, :UNIT].astype(jnp.float32)
    qdocs = jnp.broadcast_to(meta[0][:, None], (UNIT, BLK))
    lists = jnp.stack([meta[1, :64], meta[1, BLK : BLK + 64]])

    def near_id(s):
        return jnp.where(z >= s, chip - s, jnp.where(x >= 2, chip - s - NZ, -1))

    def far_id(s):
        return jnp.where(
            z + s < NZ, jnp.where(x >= 2, chip - 2 * NZ + s, -1), chip + s - NZ
        )

    def mid_id(s):
        return jnp.where(x >= 1, (x - 1) * NZ + lax.rem(z + s + NZ, NZ), -1)

    groups = [
        [(chip, -1), (near_id(1), mid_id(0))],
        [(far_id(0), mid_id(1)), (near_id(2), mid_id(-1))],
        [(far_id(1), mid_id(2)), (near_id(3), mid_id(-2))],
        [(far_id(2), mid_id(3)), (near_id(4), mid_id(-3))],
        [(far_id(3), mid_id(4))],
    ]
    ids = jnp.stack([jnp.where(core == 0, a, b) for group in groups for a, b in group])
    cols = 2 * ids[:, None] + jnp.stack([core, 1 - core])[None, :]
    cols = jnp.where(ids[:, None] >= 0, cols, -1)
    hot = cols[:, None, :, None] == jnp.arange(64, dtype=jnp.int32)[None, None, None, :]
    table = jnp.sum(jnp.where(hot, lists[None, :, None, :], 0.0), axis=-1)
    table = table.astype(jnp.int32).reshape(ids.shape[0], 4)

    core1 = core.reshape(1)

    def step(state, first, units, last=False):
        flags = table[first : first + len(units)]
        return attend_call(core1, flags, queries, qdocs, units, state, last)

    state = step(None, 0, [(unit,), (up[0],)])
    seed, sigmoid, state = lax.optimization_barrier((seed, sigmoid, state))
    down = [send(jnp.where(core == 0, seed, lead), DOWN[0])]
    up.append(send(up[1], UP[2]))
    state = step(state, 2, [(seed, lead), (up[1],)])
    for s in range(2):
        down.append(send(down[s], DOWN[s + 1]))
        if s == 0:
            up.append(send(up[2], UP[3]))
        state = step(state, 4 + 2 * s, [(down[s],), (up[s + 2],)])
    acc, stats, share, share_stats = step(state, 8, [(down[2],)], last=True)
    return combine_call(acc, stats, send(share, SWAP), send(share_stats, SWAP), sigmoid)


def solution(mesh):
    return jax.shard_map(
        on_device,
        mesh=mesh,
        in_specs=(
            P(("dp", "cp"), None),
            P(("dp", "cp"), None),
            P(("dp", "cp"), None),
            P(("dp", "cp"), None),
            P(("dp", "cp")),
            P(("dp", "cp"), None),
        ),
        out_specs=P(("dp", "cp"), None),
        check_vma=False,
    )
```

```python
import functools
import math

import jax
import jax.numpy as jnp
from jax import lax
from jax.experimental import pallas as pl
from jax.experimental.pallas import tpu as pltpu
from jax.sharding import PartitionSpec as P

H = 16
KVH = 2
HD = 256
BLK = 128
GROUPS = H // KVH
NX, NZ = 4, 8
UNIT = 2 * BLK
META = 16
WIDE = KVH * HD
LOG2E = 1.4426950408889634
NEG = -1e30


CHIPS = [(x, z) for x in range(NX) for z in range(NZ)]


def pairs_of(core, links):
    return [
        ((ax * NZ + az) * 2 + core, (bx * NZ + bz) * 2 + core)
        for (ax, az), (bx, bz) in sorted(links)
    ]


def chain_plan(seed, source, visible, length):
    wanted = [set() for _ in range(length + 1)]
    for s in range(length, -1, -1):
        wanted[s] |= {chip for chip in CHIPS if visible(*chip, s)}
        if s:
            wanted[s - 1] |= {source(*chip) for chip in wanted[s]}
    first = {(seed(*chip), chip) for chip in wanted[0]} if seed else set()
    hops = [first]
    for s in range(1, length + 1):
        hops.append({(source(*chip), chip) for chip in wanted[s]})
    return hops


NEAR = chain_plan(
    None,
    lambda x, z: (x, z - 1) if z else ((x - 2) % NX, NZ - 1),
    lambda x, z, s: z >= s or x >= 2,
    4,
)
FAR = chain_plan(
    lambda x, z: ((x + 2) % NX, z),
    lambda x, z: (x, z + 1) if z < NZ - 1 else ((x + 2) % NX, 0),
    lambda x, z, s: z + s >= NZ or x >= 2,
    3,
)
MID_UP = chain_plan(
    lambda x, z: (x - 1, z), lambda x, z: (x, (z - 1) % NZ), lambda x, z, s: x >= 1, 3
)
MID_DOWN = chain_plan(
    None, lambda x, z: (x, (z + 1) % NZ), lambda x, z, s: x >= 1, 4
)
SWAP = [(i, i ^ 1) for i in range(2 * NX * NZ)]
MID_UP[0] |= {(((x - 2) % NX, z), ((x - 1) % NX, z)) for _, (x, z) in FAR[0]}
UP = [pairs_of(0, NEAR[s]) + pairs_of(1, MID_UP[s - 1]) for s in range(1, 5)]
SEED = [
    ((((x - 1) % NX) * NZ + z) * 2 + 1, (x * NZ + z) * 2) for _, (x, z) in sorted(FAR[0])
]
LEAD = pairs_of(1, MID_DOWN[1])
DOWN = [pairs_of(0, FAR[s]) + pairs_of(1, MID_DOWN[s + 1]) for s in range(1, 4)]


def attend(first, last, paired, *refs):
    flags, core, qdocs, q_mine, q_other = refs[:5]
    rest = list(refs[5:])
    units = []
    for j, two in enumerate(paired):
        if two:
            units.append(jnp.where(core[0] == 1, rest[1][...], rest[0][...]))
        else:
            units.append(rest[0])
        rest = rest[2 if two else 1 :]
    count = len(paired)
    if not first:
        m_in, l_in, acc_in = rest[:3]
        rest = rest[3:]
    spot = lax.broadcasted_iota(jnp.int32, (BLK, BLK), 1)
    if last:
        acc_out, stats_out, share_out, share_stats_out = rest[:4]
        stats = jnp.zeros((BLK, BLK), jnp.float32)
        share_stats = jnp.zeros((BLK, BLK), jnp.float32)
    else:
        m_out, l_out, acc_out = rest[:3]
    me = core[0]
    lane = lax.broadcasted_iota(jnp.int32, (1, UNIT), 1)
    biases = []
    for j in range(count):
        kd = units[j][UNIT : UNIT + META, :UNIT].astype(jnp.float32)[0:1, :]
        halves = []
        for r in range(2):
            listed = jnp.where(lane < BLK, flags[j, 2 * r], flags[j, 2 * r + 1])
            kd_r = jnp.where(listed == 1, kd, -1.0)
            qd = qdocs[r * BLK : (r + 1) * BLK, :]
            qd = jnp.concatenate([qd, qd], axis=1)
            seen = qd == kd_r
            if first and j == 0:
                col = lax.broadcasted_iota(jnp.int32, (BLK, UNIT), 1)
                row = lax.broadcasted_iota(jnp.int32, (BLK, UNIT), 0)
                low = jnp.where(me == 0, col, lax.rem(col + BLK, UNIT))
                place = row + jnp.where(me == r, 0, BLK)
                seen = seen & (low <= place)
            halves.append(jnp.where(seen, 0.0, NEG))
        biases.append(jnp.concatenate(halves, axis=0))
    scale = LOG2E / math.sqrt(HD)
    for h in range(H):
        at = slice(h * HD, (h + 1) * HD)
        kv = slice(h // GROUPS * HD, (h // GROUPS + 1) * HD)
        qh = jnp.concatenate([q_mine[:, at], q_other[:, at]], axis=0)
        scores = []
        for j in range(count):
            s = lax.dot_general(
                qh,
                units[j][0:UNIT, kv],
                (((1,), (1,)), ((), ())),
                preferred_element_type=jnp.float32,
            )
            scores.append(s * scale + biases[j])
        top = scores[0]
        for s in scores[1:]:
            top = jnp.maximum(top, s)
        top = jnp.max(top, axis=1, keepdims=True)
        if first:
            m_new = jnp.broadcast_to(top, (UNIT, BLK))
        else:
            m_old = m_in[h]
            m_new = jnp.maximum(m_old, top)
            alpha = jnp.exp2(m_old - m_new)
        m_wide = jnp.concatenate([m_new, m_new], axis=1)
        total = None
        product = None
        for j in range(count):
            p = jnp.exp2(scores[j] - m_wide)
            part = p[:, :BLK] + p[:, BLK:]
            total = part if total is None else total + part
            pv = jnp.dot(
                p.astype(jnp.bfloat16),
                units[j][UNIT + META :, kv],
                preferred_element_type=jnp.float32,
            )
            product = pv if product is None else product + pv
        if not first:
            total = total + alpha * l_in[h]
            wide = jnp.concatenate([alpha, alpha], axis=1)
            product = product + wide * acc_in[h]
        if last:
            total = jnp.sum(total, axis=1, keepdims=True)
            acc_out[h] = product[:BLK]
            share_out[h] = (product[BLK:] / total[BLK:]).astype(jnp.bfloat16)
            stats = jnp.where(spot == h, m_new[:BLK], stats)
            stats = jnp.where(spot == H + h, total[:BLK], stats)
            share_stats = jnp.where(spot == h, m_new[BLK:], share_stats)
            share_stats = jnp.where(spot == H + h, total[BLK:], share_stats)
        else:
            m_out[h] = m_new
            l_out[h] = total
            acc_out[h] = product
    if last:
        stats_out[...] = stats
        share_stats_out[...] = share_stats


def attend_call(core, flags, queries, qdocs, units, state, last):
    paired = tuple(len(u) == 2 for u in units)
    smem = pl.BlockSpec(memory_space=pltpu.SMEM)
    vmem = pl.BlockSpec(memory_space=pltpu.VMEM)
    args = [flags, core, qdocs, *queries, *[v for u in units for v in u]]
    aliases = {}
    if state is not None:
        if not last:
            aliases = {len(args) + i: i for i in range(3)}
        args += list(state)
    if last:
        shapes = [
            jax.ShapeDtypeStruct((H, BLK, HD), jnp.float32),
            jax.ShapeDtypeStruct((BLK, BLK), jnp.float32),
            jax.ShapeDtypeStruct((H, BLK, HD), jnp.bfloat16),
            jax.ShapeDtypeStruct((BLK, BLK), jnp.float32),
        ]
    else:
        shapes = [
            jax.ShapeDtypeStruct((H, UNIT, BLK), jnp.float32),
            jax.ShapeDtypeStruct((H, UNIT, BLK), jnp.float32),
            jax.ShapeDtypeStruct((H, UNIT, HD), jnp.float32),
        ]
    return pl.pallas_call(
        functools.partial(attend, state is None, last, paired),
        out_shape=shapes,
        in_specs=[smem, smem] + [vmem] * (len(args) - 2),
        out_specs=[vmem] * len(shapes),
        input_output_aliases=aliases,
        compiler_params=pltpu.CompilerParams(vmem_limit_bytes=24 << 20),
        cost_estimate=pl.CostEstimate(
            flops=12 * H * UNIT * UNIT * HD * len(units),
            bytes_accessed=len(units) * 540000 + 9000000,
            transcendentals=H * UNIT * UNIT * len(units),
        ),
    )(*args)


def gate_sigmoid(gate, out):
    for h in range(H):
        at = slice(h * HD, (h + 1) * HD)
        out[:, at] = jax.nn.sigmoid(gate[:, at].astype(jnp.float32))


def sigmoid_call(gate_rows):
    vmem = pl.BlockSpec(memory_space=pltpu.VMEM)
    return pl.pallas_call(
        gate_sigmoid,
        out_shape=jax.ShapeDtypeStruct(gate_rows.shape, jnp.float32),
        in_specs=[vmem],
        out_specs=vmem,
        cost_estimate=pl.CostEstimate(
            flops=2000000000, bytes_accessed=3000000, transcendentals=1000000
        ),
    )(gate_rows)


def combine(acc, stats, share, share_stats, sigmoid, out):
    m0, m1 = stats[...], share_stats[...]
    l0, l1 = (pltpu.roll(v, BLK - H, 1) for v in (m0, m1))
    top = jnp.maximum(m0, m1)
    e0 = jnp.exp2(m0 - top)
    e1 = jnp.exp2(m1 - top) * l1
    inv = 1.0 / (l0 * e0 + e1)
    w0, w1 = e0 * inv, e1 * inv
    for h in range(H):
        at = slice(h * HD, (h + 1) * HD)
        att = acc[h] * w0[:, h : h + 1] + share[h].astype(jnp.float32) * w1[:, h : h + 1]
        out[:, at] = (att * sigmoid[:, at]).astype(jnp.bfloat16)


def combine_call(*args):
    vmem = pl.BlockSpec(memory_space=pltpu.VMEM)
    return pl.pallas_call(
        combine,
        out_shape=jax.ShapeDtypeStruct((BLK, H * HD), jnp.bfloat16),
        in_specs=[vmem] * len(args),
        out_specs=vmem,
        compiler_params=pltpu.CompilerParams(vmem_limit_bytes=24 << 20),
    )(*args)


def on_device(query_rows, key_rows, value_rows, gate_rows, doc_ids, block_lists):
    place = lax.axis_index("cp")
    core = lax.rem(place, 2)
    chip = place // 2
    x, z = chip // NZ, lax.rem(chip, NZ)

    def send(value, pairs):
        return lax.ppermute(value, "cp", pairs)

    docs_row = doc_ids.astype(jnp.bfloat16).reshape(1, BLK)
    lists_row = jnp.pad(
        block_lists.astype(jnp.bfloat16), ((0, 0), (0, BLK - block_lists.shape[1]))
    )
    notes = jnp.concatenate(
        [docs_row, lists_row, jnp.zeros((META - 2, BLK), jnp.bfloat16)], axis=0
    )
    notes_wide = jnp.pad(notes, ((0, 0), (0, WIDE - BLK)))
    parcel = jnp.concatenate([key_rows, value_rows, notes_wide], axis=0)
    got = send(parcel, SWAP)
    unit = jnp.concatenate(
        [
            key_rows,
            got[:BLK],
            jnp.concatenate(
                [notes, got[2 * BLK :, :BLK], jnp.zeros((META, WIDE - UNIT), jnp.bfloat16)],
                axis=1,
            ),
            value_rows,
            got[BLK : 2 * BLK],
        ],
        axis=0,
    )
    query_rows, _ = lax.optimization_barrier((query_rows, parcel))
    queries = (query_rows, send(query_rows, SWAP))

    up = [send(unit, UP[0])]
    seed = send(up[0], SEED)
    up.append(send(up[0], UP[1]))
    lead = send(up[0], LEAD)
    gate_rows, _ = lax.optimization_barrier((gate_rows, unit))
    sigmoid = sigmoid_call(gate_rows)

    meta = unit[UNIT : UNIT + 2, :UNIT].astype(jnp.float32)
    qdocs = jnp.broadcast_to(meta[0][:, None], (UNIT, BLK))
    lists = jnp.stack([meta[1, :64], meta[1, BLK : BLK + 64]])

    def near_id(s):
        return jnp.where(z >= s, chip - s, jnp.where(x >= 2, chip - s - NZ, -1))

    def far_id(s):
        return jnp.where(
            z + s < NZ, jnp.where(x >= 2, chip - 2 * NZ + s, -1), chip + s - NZ
        )

    def mid_id(s):
        return jnp.where(x >= 1, (x - 1) * NZ + lax.rem(z + s + NZ, NZ), -1)

    groups = [
        [(chip, -1, 0), (near_id(1), mid_id(0), 0)],
        [(far_id(0), mid_id(1), 1), (near_id(2), mid_id(-1), 0)],
        [(far_id(1), mid_id(2), 1), (near_id(3), mid_id(-2), 0)],
        [(far_id(2), mid_id(3), 1), (near_id(4), mid_id(-3), 0)],
        [(far_id(3), mid_id(4), 1)],
    ]
    ids = jnp.stack([jnp.where(core == 0, a, b) for group in groups for a, b, _ in group])
    turned = jnp.array([t for group in groups for _, _, t in group], jnp.int32)
    front = jnp.where(core == 0, turned, 1)
    cols = 2 * ids[:, None] + jnp.stack([front, 1 - front], axis=1)
    cols = jnp.where(ids[:, None] >= 0, cols, -1)
    hot = cols[:, None, :, None] == jnp.arange(64, dtype=jnp.int32)[None, None, None, :]
    table = jnp.sum(jnp.where(hot, lists[None, :, None, :], 0.0), axis=-1)
    table = table.astype(jnp.int32).reshape(ids.shape[0], 4)

    core1 = core.reshape(1)

    def step(state, first, units, last=False):
        flags = table[first : first + len(units)]
        return attend_call(core1, flags, queries, qdocs, units, state, last)

    state = step(None, 0, [(unit,), (up[0],)])
    seed, sigmoid, state = lax.optimization_barrier((seed, sigmoid, state))
    down = [send(jnp.where(core == 0, seed, lead), DOWN[0])]
    up.append(send(up[1], UP[2]))
    state = step(state, 2, [(seed, lead), (up[1],)])
    for s in range(2):
        down.append(send(down[s], DOWN[s + 1]))
        if s == 0:
            up.append(send(up[2], UP[3]))
        state = step(state, 4 + 2 * s, [(down[s],), (up[s + 2],)])
    acc, stats, share, share_stats = step(state, 8, [(down[2],)], last=True)
    return combine_call(acc, stats, send(share, SWAP), send(share_stats, SWAP), sigmoid)


def solution(mesh):
    return jax.shard_map(
        on_device,
        mesh=mesh,
        in_specs=(
            P(("dp", "cp"), None),
            P(("dp", "cp"), None),
            P(("dp", "cp"), None),
            P(("dp", "cp"), None),
            P(("dp", "cp")),
            P(("dp", "cp"), None),
        ),
        out_specs=P(("dp", "cp"), None),
        check_vma=False,
    )
```

```python
import functools
import math

import jax
import jax.numpy as jnp
from jax import lax
from jax.experimental import pallas as pl
from jax.experimental.pallas import tpu as pltpu
from jax.sharding import PartitionSpec as P

H = 16
KVH = 2
HD = 256
BLK = 128
GROUPS = H // KVH
NX, NZ = 4, 8
UNIT = 2 * BLK
META = 16
ROWS = GROUPS * UNIT
HALF = GROUPS * HD
LOG2E = 1.4426950408889634
NEG = -1e30


def permutation(target):
    pairs = []
    for x in range(NX):
        for z in range(NZ):
            for core in range(2):
                goal = target(x, z, core)
                if goal is not None:
                    gx, gz, gc = goal
                    pairs.append(((x * NZ + z) * 2 + core, (gx * NZ + gz) * 2 + gc))
    return pairs


SWAP = permutation(lambda x, z, c: (x, z, 1 - c))
ONE_X = permutation(lambda x, z, c: (x + 1, z, c) if x < 3 else None)
TWO_X = permutation(lambda x, z, c: ((x + 2) % NX, z, c))
NEAR_UP = permutation(
    lambda x, z, c: (x, z + 1, c) if z < 7 else ((x + 2, 0, c) if x < 2 else None)
)
NEAR_DOWN = permutation(
    lambda x, z, c: (x, z - 1, c) if z > 0 else ((x + 2) % NX, 7, c)
)
MID_UP = permutation(lambda x, z, c: (x, (z + 1) % NZ, c) if x > 0 else None)
MID_DOWN = permutation(lambda x, z, c: (x, (z - 1) % NZ, c) if x > 0 else None)


def attend(own_at, last, count, *refs):
    flags, core, q, qdocs = refs[:4]
    units = refs[4 : 4 + count]
    rest = list(refs[4 + count :])
    first = own_at is not None
    if not first:
        m_in, l_in, acc_in = rest[:3]
        rest = rest[3:]
    if last:
        gate_mine, gate_other = rest[:2]
        rest = rest[2:]
        out_mine, out_other = rest[:2]
    else:
        m_out, l_out, acc_out = rest[:3]
        rest = rest[3:]
    me = core[0]
    lane = lax.broadcasted_iota(jnp.int32, (1, UNIT), 1)
    biases = []
    for j in range(count):
        kd = units[j][UNIT : UNIT + META, :].astype(jnp.float32)[0:1, :]
        halves = []
        for r in range(2):
            listed = jnp.where(lane < BLK, flags[j, 2 * r], flags[j, 2 * r + 1])
            kd_r = jnp.where(listed == 1, kd, -1.0)
            qd = qdocs[r * BLK : (r + 1) * BLK, :]
            qd = jnp.concatenate([qd, qd], axis=1)
            seen = qd == kd_r
            if own_at == j:
                col = lax.broadcasted_iota(jnp.int32, (BLK, UNIT), 1)
                row = lax.broadcasted_iota(jnp.int32, (BLK, UNIT), 0)
                low = jnp.where(me == 0, col, lax.rem(col + BLK, UNIT))
                place = row + jnp.where(me == r, 0, BLK)
                seen = seen & (low <= place)
            halves.append(jnp.where(seen, 0.0, NEG))
        biases.append(jnp.concatenate(halves, axis=0))
    scale = LOG2E / math.sqrt(HD)
    for h in range(GROUPS):
        qh = q[h * UNIT : (h + 1) * UNIT, :]
        scores = []
        for j in range(count):
            s = lax.dot_general(
                qh,
                units[j][0:UNIT, :],
                (((1,), (1,)), ((), ())),
                preferred_element_type=jnp.float32,
            )
            scores.append(s * scale + biases[j])
        top = scores[0]
        for s in scores[1:]:
            top = jnp.maximum(top, s)
        top = jnp.max(top, axis=1, keepdims=True)
        if first:
            m_new = jnp.broadcast_to(top, (UNIT, BLK))
        else:
            m_old = m_in[h]
            m_new = jnp.maximum(m_old, top)
            alpha = jnp.exp2(m_old - m_new)
        m_wide = jnp.concatenate([m_new, m_new], axis=1)
        total = None
        product = None
        for j in range(count):
            p = jnp.exp2(scores[j] - m_wide)
            part = p[:, :BLK] + p[:, BLK:]
            total = part if total is None else total + part
            pv = jnp.dot(
                p.astype(jnp.bfloat16),
                units[j][UNIT + META :, :],
                preferred_element_type=jnp.float32,
            )
            product = pv if product is None else product + pv
        if not first:
            total = total + alpha * l_in[h]
            wide = jnp.concatenate([alpha, alpha], axis=1)
            product = product + wide * acc_in[h]
        if last:
            inv = 1.0 / jnp.sum(total, axis=1, keepdims=True)
            att = product * inv
            base = pl.multiple_of(me * HALF + h * HD, HD)
            g = gate_mine[:, pl.ds(base, HD)].astype(jnp.float32)
            out_mine[:, h * HD : (h + 1) * HD] = (
                att[:BLK] * jax.nn.sigmoid(g)
            ).astype(jnp.bfloat16)
            g = gate_other[:, h * HD : (h + 1) * HD].astype(jnp.float32)
            out_other[:, h * HD : (h + 1) * HD] = (
                att[BLK:] * jax.nn.sigmoid(g)
            ).astype(jnp.bfloat16)
        else:
            m_out[h] = m_new
            l_out[h] = total
            acc_out[h] = product


def attend_call(core, flags, q, qdocs, units, state=None, gates=None, own_at=None):
    count = len(units)
    last = gates is not None
    smem = pl.BlockSpec(memory_space=pltpu.SMEM)
    vmem = pl.BlockSpec(memory_space=pltpu.VMEM)
    args = [flags, core, q, qdocs, *units]
    aliases = {}
    if state is not None:
        if not last:
            aliases = {len(args) + i: i for i in range(3)}
        args += list(state)
    if last:
        args += list(gates)
        shapes = [jax.ShapeDtypeStruct((BLK, HALF), jnp.bfloat16)] * 2
    else:
        shapes = [
            jax.ShapeDtypeStruct((GROUPS, UNIT, BLK), jnp.float32),
            jax.ShapeDtypeStruct((GROUPS, UNIT, BLK), jnp.float32),
            jax.ShapeDtypeStruct((GROUPS, UNIT, HD), jnp.float32),
        ]
    specs = [smem, smem] + [vmem] * (len(args) - 2)
    return pl.pallas_call(
        functools.partial(attend, own_at, last, count),
        out_shape=shapes,
        in_specs=specs,
        out_specs=[vmem] * len(shapes),
        input_output_aliases=aliases,
        compiler_params=pltpu.CompilerParams(vmem_limit_bytes=32 << 20),
        cost_estimate=pl.CostEstimate(
            flops=4 * ROWS * UNIT * HD * count,
            bytes_accessed=count * 270000 + 9000000,
            transcendentals=ROWS * UNIT * count,
        ),
    )(*args)


def on_device(query_rows, key_rows, value_rows, gate_rows, doc_ids, block_lists):
    place = lax.axis_index("cp")
    core = lax.rem(place, 2)
    chip = place // 2
    x, z = chip // NZ, lax.rem(chip, NZ)

    def send(value, pairs):
        return lax.ppermute(value, "cp", pairs)

    def take(rows, which, width):
        return lax.dynamic_slice_in_dim(rows, which * width, width, 1)

    docs_row = doc_ids.astype(jnp.bfloat16).reshape(1, BLK)
    lists_row = jnp.pad(
        block_lists.astype(jnp.bfloat16), ((0, 0), (0, BLK - block_lists.shape[1]))
    )
    notes = jnp.concatenate(
        [docs_row, lists_row, jnp.zeros((META - 2, BLK), jnp.bfloat16)], axis=0
    )
    notes_wide = jnp.concatenate([notes, jnp.zeros_like(notes)], axis=1)
    parcel = jnp.concatenate(
        [take(key_rows, 1 - core, HD), take(value_rows, 1 - core, HD), notes_wide], axis=0
    )
    got = send(parcel, SWAP)
    unit = jnp.concatenate(
        [
            take(key_rows, core, HD),
            got[:BLK],
            jnp.concatenate([notes, got[2 * BLK :, :BLK]], axis=1),
            take(value_rows, core, HD),
            got[BLK : 2 * BLK],
        ],
        axis=0,
    )
    up = [unit]
    mid0 = send(unit, ONE_X)
    low0 = send(unit, TWO_X)
    down = [low0]
    mup, mdown = [mid0], [mid0]
    for s in range(4):
        up.append(send(up[-1], NEAR_UP))
        mup.append(send(mup[-1], MID_UP))
        if s < 3:
            down.append(send(down[-1], NEAR_DOWN))
            mdown.append(send(mdown[-1], MID_DOWN))

    query_rows, gate_rows, _ = lax.optimization_barrier((query_rows, gate_rows, unit))
    q_other = send(take(query_rows, 1 - core, HALF), SWAP)
    gate_other = send(take(gate_rows, 1 - core, HALF), SWAP)
    q = jnp.concatenate([take(query_rows, core, HALF), q_other], axis=0)
    q = q.reshape(UNIT, GROUPS, HD).transpose(1, 0, 2).reshape(ROWS, HD)
    meta = unit[UNIT : UNIT + 2].astype(jnp.float32)
    qdocs = jnp.broadcast_to(meta[0][:, None], (UNIT, BLK))
    lists = jnp.stack([meta[1, :64], meta[1, BLK : BLK + 64]])

    def up_id(s):
        return jnp.where(z >= s, chip - s, jnp.where(x >= 2, chip - s - NZ, -1))

    def down_id(s):
        return jnp.where(
            z + s < NZ, jnp.where(x >= 2, chip - 2 * NZ + s, -1), chip + s - NZ
        )

    def mid_id(s):
        return jnp.where(x >= 1, (x - 1) * NZ + lax.rem(z + s + NZ, NZ), -1)

    groups = [
        [(up[0], chip)],
        [(up[1], up_id(1)), (down[0], down_id(0)), (mup[0], mid_id(0))],
        [(up[2], up_id(2)), (down[1], down_id(1)), (mup[1], mid_id(-1)), (mdown[1], mid_id(1))],
        [(up[3], up_id(3)), (down[2], down_id(2)), (mup[2], mid_id(-2)), (mdown[2], mid_id(2))],
        [
            (up[4], up_id(4)),
            (down[3], down_id(3)),
            (mup[3], mid_id(-3)),
            (mdown[3], mid_id(3)),
            (mup[4], mid_id(-4)),
        ],
    ]
    ids = jnp.stack([i for group in groups for _, i in group])
    cols = 2 * ids[:, None] + jnp.stack([core, 1 - core])[None, :]
    cols = jnp.where(ids[:, None] >= 0, cols, -1)
    hot = cols[:, None, :, None] == jnp.arange(64, dtype=jnp.int32)[None, None, None, :]
    table = jnp.sum(jnp.where(hot, lists[None, :, None, :], 0.0), axis=-1)
    table = table.astype(jnp.int32).reshape(ids.shape[0], 4)

    core1 = core.reshape(1)
    state = None
    at = 0
    for n, group in enumerate(groups):
        flags = table[at : at + len(group)]
        at += len(group)
        gates = (gate_rows, gate_other) if n == len(groups) - 1 else None
        state = attend_call(
            core1, flags, q, qdocs, [u for u, _ in group], state, gates, 0 if n == 0 else None
        )
    mine, other = state
    back = send(other, SWAP)
    return jnp.where(
        core == 0,
        jnp.concatenate([mine, back], axis=1),
        jnp.concatenate([back, mine], axis=1),
    )


def solution(mesh):
    return jax.shard_map(
        on_device,
        mesh=mesh,
        in_specs=(
            P(("dp", "cp"), None),
            P(("dp", "cp"), None),
            P(("dp", "cp"), None),
            P(("dp", "cp"), None),
            P(("dp", "cp")),
            P(("dp", "cp"), None),
        ),
        out_specs=P(("dp", "cp"), None),
        check_vma=False,
    )
```

```python
import functools
import math

import jax
import jax.numpy as jnp
from jax import lax
from jax.experimental import pallas as pl
from jax.experimental.pallas import tpu as pltpu
from jax.sharding import PartitionSpec as P

H = 16
KVH = 2
HD = 256
BLK = 128
GROUPS = H // KVH
NX, NZ = 4, 8
UNIT = 2 * BLK
META = 16
ROWS = GROUPS * UNIT
HALF = GROUPS * HD
LOG2E = 1.4426950408889634
NEG = -1e30


def permutation(target):
    pairs = []
    for x in range(NX):
        for z in range(NZ):
            for core in range(2):
                goal = target(x, z, core)
                if goal is not None:
                    gx, gz, gc = goal
                    pairs.append(((x * NZ + z) * 2 + core, (gx * NZ + gz) * 2 + gc))
    return pairs


SWAP = permutation(lambda x, z, c: (x, z, 1 - c))
ONE_X = permutation(lambda x, z, c: (x + 1, z, c) if x < 3 else None)
TWO_X = permutation(lambda x, z, c: ((x + 2) % NX, z, c))
NEAR_UP = permutation(
    lambda x, z, c: (x, z + 1, c) if z < 7 else ((x + 2, 0, c) if x < 2 else None)
)
NEAR_DOWN = permutation(
    lambda x, z, c: (x, z - 1, c) if z > 0 else ((x + 2) % NX, 7, c)
)
MID_UP = permutation(lambda x, z, c: (x, (z + 1) % NZ, c) if x > 0 else None)
MID_DOWN = permutation(lambda x, z, c: (x, (z - 1) % NZ, c) if x > 0 else None)


def attend(own_at, last, count, *refs):
    flags, core, q, qdocs = refs[:4]
    units = refs[4 : 4 + count]
    rest = list(refs[4 + count :])
    first = own_at is not None
    if not first:
        m_in, l_in, acc_in = rest[:3]
        rest = rest[3:]
    if last:
        gate_mine, gate_other = rest[:2]
        rest = rest[2:]
        out_mine, out_other = rest[:2]
    else:
        m_out, l_out, acc_out = rest[:3]
        rest = rest[3:]
    me = core[0]
    lane = lax.broadcasted_iota(jnp.int32, (1, UNIT), 1)
    biases = []
    for j in range(count):
        kd = units[j][UNIT : UNIT + META, :].astype(jnp.float32)[0:1, :]
        halves = []
        for r in range(2):
            listed = jnp.where(lane < BLK, flags[j, 2 * r], flags[j, 2 * r + 1])
            kd_r = jnp.where(listed == 1, kd, -1.0)
            qd = qdocs[r * BLK : (r + 1) * BLK, :]
            qd = jnp.concatenate([qd, qd], axis=1)
            seen = qd == kd_r
            if own_at == j:
                col = lax.broadcasted_iota(jnp.int32, (BLK, UNIT), 1)
                row = lax.broadcasted_iota(jnp.int32, (BLK, UNIT), 0)
                low = jnp.where(me == 0, col, lax.rem(col + BLK, UNIT))
                place = row + jnp.where(me == r, 0, BLK)
                seen = seen & (low <= place)
            halves.append(jnp.where(seen, 0.0, NEG))
        biases.append(jnp.concatenate(halves, axis=0))
    scale = LOG2E / math.sqrt(HD)
    for h in range(GROUPS):
        qh = q[h * UNIT : (h + 1) * UNIT, :]
        scores = []
        for j in range(count):
            s = lax.dot_general(
                qh,
                units[j][0:UNIT, :],
                (((1,), (1,)), ((), ())),
                preferred_element_type=jnp.float32,
            )
            scores.append(s * scale + biases[j])
        top = scores[0]
        for s in scores[1:]:
            top = jnp.maximum(top, s)
        top = jnp.max(top, axis=1, keepdims=True)
        if first:
            m_new = jnp.broadcast_to(top, (UNIT, BLK))
        else:
            m_old = m_in[h]
            m_new = jnp.maximum(m_old, top)
            alpha = jnp.exp2(m_old - m_new)
        m_wide = jnp.concatenate([m_new, m_new], axis=1)
        total = None
        product = None
        for j in range(count):
            p = jnp.exp2(scores[j] - m_wide)
            part = p[:, :BLK] + p[:, BLK:]
            total = part if total is None else total + part
            pv = jnp.dot(
                p.astype(jnp.bfloat16),
                units[j][UNIT + META :, :],
                preferred_element_type=jnp.float32,
            )
            product = pv if product is None else product + pv
        if not first:
            total = total + alpha * l_in[h]
            wide = jnp.concatenate([alpha, alpha], axis=1)
            product = product + wide * acc_in[h]
        if last:
            inv = 1.0 / jnp.sum(total, axis=1, keepdims=True)
            att = product * inv
            base = pl.multiple_of(me * HALF + h * HD, HD)
            g = gate_mine[:, pl.ds(base, HD)].astype(jnp.float32)
            out_mine[:, h * HD : (h + 1) * HD] = (
                att[:BLK] * jax.nn.sigmoid(g)
            ).astype(jnp.bfloat16)
            g = gate_other[:, h * HD : (h + 1) * HD].astype(jnp.float32)
            out_other[:, h * HD : (h + 1) * HD] = (
                att[BLK:] * jax.nn.sigmoid(g)
            ).astype(jnp.bfloat16)
        else:
            m_out[h] = m_new
            l_out[h] = total
            acc_out[h] = product


def attend_call(core, flags, q, qdocs, units, state=None, gates=None, own_at=None):
    count = len(units)
    last = gates is not None
    smem = pl.BlockSpec(memory_space=pltpu.SMEM)
    vmem = pl.BlockSpec(memory_space=pltpu.VMEM)
    args = [flags, core, q, qdocs, *units]
    aliases = {}
    if state is not None:
        if not last:
            aliases = {len(args) + i: i for i in range(3)}
        args += list(state)
    if last:
        args += list(gates)
        shapes = [jax.ShapeDtypeStruct((BLK, HALF), jnp.bfloat16)] * 2
    else:
        shapes = [
            jax.ShapeDtypeStruct((GROUPS, UNIT, BLK), jnp.float32),
            jax.ShapeDtypeStruct((GROUPS, UNIT, BLK), jnp.float32),
            jax.ShapeDtypeStruct((GROUPS, UNIT, HD), jnp.float32),
        ]
    specs = [smem, smem] + [vmem] * (len(args) - 2)
    return pl.pallas_call(
        functools.partial(attend, own_at, last, count),
        out_shape=shapes,
        in_specs=specs,
        out_specs=[vmem] * len(shapes),
        input_output_aliases=aliases,
        compiler_params=pltpu.CompilerParams(vmem_limit_bytes=32 << 20),
        cost_estimate=pl.CostEstimate(
            flops=4 * ROWS * UNIT * HD * count,
            bytes_accessed=count * 270000 + 9000000,
            transcendentals=ROWS * UNIT * count,
        ),
    )(*args)


def on_device(query_rows, key_rows, value_rows, gate_rows, doc_ids, block_lists):
    place = lax.axis_index("cp")
    core = lax.rem(place, 2)
    chip = place // 2
    x, z = chip // NZ, lax.rem(chip, NZ)

    def send(value, pairs):
        return lax.ppermute(value, "cp", pairs)

    def take(rows, which, width):
        return lax.dynamic_slice_in_dim(rows, which * width, width, 1)

    docs_row = doc_ids.astype(jnp.bfloat16).reshape(1, BLK)
    lists_row = jnp.pad(
        block_lists.astype(jnp.bfloat16), ((0, 0), (0, BLK - block_lists.shape[1]))
    )
    notes = jnp.concatenate(
        [docs_row, lists_row, jnp.zeros((META - 2, BLK), jnp.bfloat16)], axis=0
    )
    notes_wide = jnp.concatenate([notes, jnp.zeros_like(notes)], axis=1)
    parcel = jnp.concatenate(
        [take(key_rows, 1 - core, HD), take(value_rows, 1 - core, HD), notes_wide], axis=0
    )
    got = send(parcel, SWAP)
    unit = jnp.concatenate(
        [
            take(key_rows, core, HD),
            got[:BLK],
            jnp.concatenate([notes, got[2 * BLK :, :BLK]], axis=1),
            take(value_rows, core, HD),
            got[BLK : 2 * BLK],
        ],
        axis=0,
    )
    up = [unit]
    mid0 = send(unit, ONE_X)
    low0 = send(unit, TWO_X)
    down = [low0]
    mup, mdown = [mid0], [mid0]
    for s in range(4):
        up.append(send(up[-1], NEAR_UP))
        mdown.append(send(mdown[-1], MID_DOWN))
        if s < 3:
            down.append(send(down[-1], NEAR_DOWN))
            mup.append(send(mup[-1], MID_UP))

    q_other = send(take(query_rows, 1 - core, HALF), SWAP)
    gate_other = send(take(gate_rows, 1 - core, HALF), SWAP)
    q = jnp.concatenate([take(query_rows, core, HALF), q_other], axis=0)
    q = q.reshape(UNIT, GROUPS, HD).transpose(1, 0, 2).reshape(ROWS, HD)
    meta = unit[UNIT : UNIT + 2].astype(jnp.float32)
    qdocs = jnp.broadcast_to(meta[0][:, None], (UNIT, BLK))
    lists = jnp.stack([meta[1, :64], meta[1, BLK : BLK + 64]])

    def up_id(s):
        return jnp.where(z >= s, chip - s, jnp.where(x >= 2, chip - s - NZ, -1))

    def down_id(s):
        return jnp.where(
            z + s < NZ, jnp.where(x >= 2, chip - 2 * NZ + s, -1), chip + s - NZ
        )

    def mid_id(s):
        return jnp.where(x >= 1, (x - 1) * NZ + lax.rem(z + s + NZ, NZ), -1)

    groups = [
        [(up[0], chip)],
        [(up[1], up_id(1)), (down[0], down_id(0)), (mup[0], mid_id(0))],
        [(up[2], up_id(2)), (down[1], down_id(1)), (mup[1], mid_id(-1)), (mdown[1], mid_id(1))],
        [(up[3], up_id(3)), (down[2], down_id(2)), (mup[2], mid_id(-2)), (mdown[2], mid_id(2))],
        [
            (up[4], up_id(4)),
            (down[3], down_id(3)),
            (mup[3], mid_id(-3)),
            (mdown[3], mid_id(3)),
            (mdown[4], mid_id(4)),
        ],
    ]
    ids = jnp.stack([i for group in groups for _, i in group])
    cols = 2 * ids[:, None] + jnp.stack([core, 1 - core])[None, :]
    cols = jnp.where(ids[:, None] >= 0, cols, -1)
    hot = cols[:, None, :, None] == jnp.arange(64, dtype=jnp.int32)[None, None, None, :]
    table = jnp.sum(jnp.where(hot, lists[None, :, None, :], 0.0), axis=-1)
    table = table.astype(jnp.int32).reshape(ids.shape[0], 4)

    core1 = core.reshape(1)
    state = None
    at = 0
    for n, group in enumerate(groups):
        flags = table[at : at + len(group)]
        at += len(group)
        gates = (gate_rows, gate_other) if n == len(groups) - 1 else None
        state = attend_call(
            core1, flags, q, qdocs, [u for u, _ in group], state, gates, 0 if n == 0 else None
        )
    mine, other = state
    back = send(other, SWAP)
    return jnp.where(
        core == 0,
        jnp.concatenate([mine, back], axis=1),
        jnp.concatenate([back, mine], axis=1),
    )


def solution(mesh):
    return jax.shard_map(
        on_device,
        mesh=mesh,
        in_specs=(
            P(("dp", "cp"), None),
            P(("dp", "cp"), None),
            P(("dp", "cp"), None),
            P(("dp", "cp"), None),
            P(("dp", "cp")),
            P(("dp", "cp"), None),
        ),
        out_specs=P(("dp", "cp"), None),
        check_vma=False,
    )
```
